128 devices in a mesh: obs: 16 (over z, y), lvl: 8 (over x, core).
Axes of the slice: x: 4, y: 4, z: 4, core: 2. Of those that a mesh axis runs over, the one named last changes fastest.
Arguments:
- rhs: float32 [64, 1048576], P(None, ('obs', 'lvl')), may hold values from -15 to 15
- tile_weights: bfloat16 [16384, 64, 128], P(('obs', 'lvl')), may hold values from -0.3125 to 0.3125
- tile_owner: int32 [16384, 1], P(('obs', 'lvl')), may hold values from 0 to 127; in each aligned block of 128 rows (0 to 127, 128 to 255, ...) at most 2 rows name the same one
- tile_row: int32 [16384], P(('obs', 'lvl')), may hold values from 0 to 7
- axis_a: bfloat16 [128, 8, 128], P('obs', 'lvl'), as said below
- axis_b: bfloat16 [8, 128, 128], P('lvl'), as said below
- coupling: float32 [8, 8], replicated, as said below
- noise: float32 [64], replicated, may hold values from 0.1 to 1
Outputs:
- solution: float32 [64, 1048576], P(None, ('obs', 'lvl'))
- residual: float32 [64, 1048576], P(None, ('obs', 'lvl'))
The draws below stay inside these ranges and needn't reach their ends.
Inputs may be any that keep to these rules, and one draw needn't show every extreme that they name: `tile_owner`: among the 128 tiles of one device no owner is named more than 2 times, a bound that some block reaches. For each level l, axis_a[x, l, a] equals axis_a[a, l, x]. For each level l, axis_b[l] is symmetric. coupling is symmetric and positive definite.
All inputs are finite; a program needn't handle non-finite values.
Results may differ from the reference program's by a relative error of at most 0.017.
Values may be sent and summed in bfloat16 or wider, within the bound.
A program may use at most 64 MiB of HBM per device.

```python
import math
import jax
import jax.numpy as jnp
import numpy as np
from jax import lax

R = 64
TB = 64
NB = 128
NA = 128
LEVELS = 8
ITERS = 2
TILE_DEV = 128
NTILES = 16384
NOBS = 1048576
CAP = 2
BLK_DEV = 8
N_OBS = 16
N_LVL = 8
DEVICES = 128


def symmetric_stack(raw, diag_key, count, order):
    sym = (raw + jnp.swapaxes(raw, 1, 2)) * (0.5 / jnp.sqrt(2.0 * order))
    diagonal = jax.random.uniform(diag_key, (count, order), jnp.float32, 1.0, 2.0)
    return sym + diagonal[:, :, None] * jnp.eye(order, dtype=jnp.float32)[None]


def draw_rhs(key, part):
    base_key = jax.random.fold_in(key, 53)
    place = jnp.arange(NOBS, dtype=jnp.float32) / NOBS
    raw = jnp.clip(jax.random.normal(base_key, (R, NOBS), jnp.float32), -6.0, 6.0)
    scale = 0.4 * jnp.exp(jnp.log(6.0) * place)
    return raw * scale[None, :]


def draw_axis_a(key, part):
    first_key, second_key = jax.random.split(jax.random.fold_in(key, 11))
    raw = jax.random.normal(first_key, (LEVELS, NA, NA), jnp.float32)
    stack = symmetric_stack(raw, second_key, LEVELS, NA)
    return jnp.transpose(stack, (1, 0, 2)).astype(jnp.bfloat16)


def draw_axis_b(key, part):
    first_key, second_key = jax.random.split(jax.random.fold_in(key, 23))
    raw = jax.random.normal(first_key, (LEVELS, NB, NB), jnp.float32)
    return symmetric_stack(raw, second_key, LEVELS, NB).astype(jnp.bfloat16)


def draw_coupling(key, part):
    inner = jax.random.normal(jax.random.fold_in(key, 37), (LEVELS, LEVELS), jnp.float32)
    return 0.5 * jnp.eye(LEVELS, dtype=jnp.float32) + jnp.dot(inner, inner.T) / LEVELS


def touch_ends(entries, stream_key, smallest, top_value):
    longest = entries.shape.index(max(entries.shape))
    spots = []
    for shift in (0, 1):
        where = [jax.random.randint(jax.random.fold_in(stream_key, axis), (), 0, length) for axis, length in enumerate(entries.shape)]
        where[longest] = (where[longest] + shift) % entries.shape[longest]
        spots.append(tuple(where))
    return entries.at[spots[0]].set(smallest).at[spots[1]].set(top_value)


def block_levels(own_key, dims, cuts, smallest, largest):
    def one(position, blocks):
        steps = jax.random.uniform(jax.random.fold_in(jax.random.fold_in(own_key, 6), position), (blocks,), jnp.float32, smallest / len(cuts), largest / len(cuts))
        return jnp.repeat(jnp.exp(steps), dims[position] // blocks).reshape((-1,) + (1,) * (len(dims) - position - 1))

    factor_of = one(*cuts[0])
    for cut in cuts[1:]:
        factor_of = factor_of * one(*cut)
    return factor_of


def routed_block(stream_key, own, number, rows, count, top, limit, slope):
    ranking = jax.random.permutation(stream_key, count)
    packed, common = shares(count, rows * top, limit, slope, True), shares(count, rows * top, limit, slope, False)
    places = jnp.arange(count)

    def named(tallies, rotation):
        used = int((tallies > 0).sum())
        fixed = max(1, used // 4)
        shifted = fixed + (places - fixed + rotation * (used - fixed)) % max(1, count - fixed)
        return jnp.zeros((count,), jnp.int32).at[ranking[jnp.where(places < fixed, places, shifted)]].set(jnp.asarray(tallies, jnp.int32))

    tallies = jnp.where(number % 4 == 0, named(packed, number // 4), named(common, number - number // 4 - 1))
    mixed = jax.random.permutation(jax.random.fold_in(own, 3), count)
    source_of, receiver = mixed[0:count // 2 * 2:2], mixed[1:count // 2 * 2:2]
    room = jnp.minimum(tallies[source_of] - 1, limit - tallies[receiver]) // 2
    room = jnp.where((source_of == ranking[0]) | (receiver == ranking[0]) | (tallies[receiver] == 0), 0, jnp.maximum(room, 0))
    shifted = jax.random.randint(jax.random.fold_in(own, 4), (count // 2,), 0, 1 << 20) % (room + 1)
    tallies = tallies.at[source_of].add(-shifted).at[receiver].add(shifted)
    members = jnp.searchsorted(jnp.cumsum(tallies), jnp.arange(rows * top), side="right").astype(jnp.int32)
    listing = members.reshape(top, rows).T
    listing = listing[jax.random.permutation(jax.random.fold_in(own, 1), rows)]
    rotation = jax.random.randint(jax.random.fold_in(own, 2), (rows, 1), 0, top)
    return jnp.take_along_axis(listing, (jnp.arange(top)[None, :] + rotation) % top, axis=1)


def shares(number_of, total, bound, slope, full):
    loads = [(1 << 20) // math.isqrt(rank ** slope) + 1 for rank in range(1, number_of + 1)]
    largest = bound if full else min(bound, max(-(-total // number_of), total * loads[0] // sum(loads)))
    least = 1 if total - largest >= number_of - 1 else 0
    given, rest = [largest] + [least] * (number_of - 1), total - largest - least * (number_of - 1)
    while rest > 0:
        movable = [i for i in range(1, number_of) if given[i] < largest] or [i for i in range(1, number_of) if given[i] < bound]
        mass, budget = sum([loads[i] for i in movable]), rest
        for i in movable:
            addition = min(bound - given[i], max(1, budget * loads[i] // mass), rest)
            given[i] = given[i] + addition
            rest = rest - addition
    return np.array(given)


def scatter_about(stream_key, dims, deviation, limit, cuts=(), kind=jnp.bfloat16):
    loudness = block_levels(stream_key, dims, cuts, -0.22, 0.18) if cuts else 1.0
    drawn = jax.random.normal(stream_key, dims, jnp.float32) * deviation * loudness
    return jnp.minimum(jnp.maximum(drawn, -limit), limit).astype(kind)


def setup_inputs(seed: int = 0) -> dict:
    splits = jax.random.split(jax.random.key(seed), 9)
    rhs = draw_rhs(jax.random.fold_in(splits[8], 71), 0)
    tile_weights = scatter_about(splits[1], (NTILES, TB, NB), (6 * TB) ** -0.5, 0.3125, ((0, 128),))
    tile_owner_keys = jax.random.split(jax.random.fold_in(splits[2], 1), NTILES // TILE_DEV)
    tile_owner_turns = jax.random.permutation(jax.random.fold_in(splits[2], 3), NTILES // TILE_DEV)
    tile_owner = jax.vmap(lambda own, number: routed_block(jax.random.fold_in(splits[2], 2), own, number, TILE_DEV, DEVICES, 1, CAP, 2))(tile_owner_keys, tile_owner_turns).reshape((NTILES, 1))
    tile_row = touch_ends(jax.random.randint(splits[3], (NTILES,), 0, BLK_DEV), jax.random.fold_in(splits[3], 1), 0, BLK_DEV - 1).astype(jnp.int32)
    axis_a = draw_axis_a(jax.random.fold_in(splits[8], 71), 0)
    axis_b = draw_axis_b(jax.random.fold_in(splits[8], 71), 0)
    coupling = draw_coupling(jax.random.fold_in(splits[8], 71), 0)
    noise = jnp.clip(jnp.exp(jax.random.uniform(splits[7], (R,), jnp.float32, math.log(0.1), math.log(1.0))), 0.1, 1.0)
    return {"rhs": rhs, "tile_weights": tile_weights, "tile_owner": tile_owner, "tile_row": tile_row, "axis_a": axis_a, "axis_b": axis_b, "coupling": coupling, "noise": noise}


def axis_pass(field, axis_a, axis_b):
    first = jnp.einsum('alrb,lbc->alrc', field.astype(jnp.float32), axis_b.astype(jnp.float32)).astype(jnp.bfloat16)
    return jnp.einsum('xla,alrc->xlrc', axis_a.astype(jnp.float32), first.astype(jnp.float32)).astype(jnp.bfloat16)


def reference(rhs, tile_weights, tile_owner, tile_row, axis_a, axis_b, coupling, noise):
    tile_count = tile_weights.shape[0]
    a_share = NA // N_OBS
    lvl_share = LEVELS // N_LVL
    owner = tile_owner[:, 0]
    a_index = (owner // N_LVL) * a_share + tile_row // lvl_share
    l_index = (owner % N_LVL) * lvl_share + tile_row % lvl_share
    flat = (a_index * LEVELS + l_index).astype(jnp.int32)
    block = math.gcd(tile_count, 1024)
    steps_count = tile_count // block
    weight_blocks = tile_weights.reshape(steps_count, block, TB, NB)
    flat_blocks = flat.reshape(steps_count, block)

    def operator(direction):
        low = direction.astype(jnp.bfloat16).reshape(R, tile_count, TB)
        low_tiles = jnp.transpose(low, (1, 0, 2)).reshape(steps_count, block, R, TB)

        def forward(total, pieces):
            values, weights, places = pieces
            part = jnp.einsum('krt,ktn->krn', values.astype(jnp.float32), weights.astype(jnp.float32)).astype(jnp.bfloat16)
            return total + jax.ops.segment_sum(part.astype(jnp.float32), places, num_segments=NA * LEVELS), None

        start = jnp.zeros((NA * LEVELS, R, NB), jnp.float32)
        node_sums, unused = lax.scan(forward, start, (low_tiles, weight_blocks, flat_blocks))
        node_sums = node_sums.astype(jnp.bfloat16).reshape(NA, LEVELS, R, NB)
        spread = axis_pass(node_sums, axis_a, axis_b)
        mixed = jnp.einsum('lm,amrc->alrc', coupling, spread.astype(jnp.float32), precision=lax.Precision.HIGHEST).astype(jnp.bfloat16)
        grid_values = axis_pass(mixed, axis_a, axis_b).reshape(NA * LEVELS, R, NB)

        def backward(carry, pieces):
            weights, places = pieces
            picked = grid_values[places].astype(jnp.float32)
            back = jnp.einsum('krn,ktn->krt', picked, weights.astype(jnp.float32)).astype(jnp.bfloat16)
            return carry, back

        unused, backs = lax.scan(backward, jnp.zeros((), jnp.float32), (weight_blocks, flat_blocks))
        backs = backs.reshape(tile_count, R, TB)
        back = jnp.transpose(backs, (1, 0, 2)).reshape(R, tile_count * TB)
        return back.astype(jnp.float32) + noise[:, None] * direction

    solution = jnp.zeros_like(rhs)
    residual = rhs
    direction = rhs
    norm_now = jnp.sum(residual * residual, axis=1)
    for step in range(ITERS):
        image = operator(direction)
        alpha = norm_now / jnp.sum(direction * image, axis=1)
        solution = solution + alpha[:, None] * direction
        residual = residual - alpha[:, None] * image
        if step + 1 < ITERS:
            norm_next = jnp.sum(residual * residual, axis=1)
            direction = residual + (norm_next / norm_now)[:, None] * direction
            norm_now = norm_next
    return solution, residual
```

```python
import jax
import jax.numpy as jnp
from jax import lax
from jax.sharding import Mesh
from jax.sharding import PartitionSpec as P

ITERS = 2
OBS_LVL = ("obs_0", "obs_1", "lvl_0", "lvl_1")
OBS = ("obs_0", "obs_1")
LVL = ("lvl_0", "lvl_1")
CHIPS = ("obs_0", "obs_1", "lvl_0")
CORE = "lvl_1"


def on_device(rhs, tile_weights, tile_owner, tile_row, axis_a, axis_b, coupling, noise):
    chips = lax.axis_size(CHIPS)
    lvl_count = lax.axis_size(LVL)
    tile_count, tile_obs, node_cols = tile_weights.shape
    columns = rhs.shape[0]
    a_rows, lvl_here, grid_first = axis_a.shape
    levels = lvl_count * lvl_here
    per_chip = columns // chips
    owner = tile_owner[:, 0]
    level = (owner % lvl_count) * lvl_here + tile_row % lvl_here
    first_index = owner // lvl_count * a_rows + tile_row // lvl_here
    place = level * grid_first + first_index
    places = lax.all_gather(place, CHIPS).reshape(chips * tile_count)
    kernel_a = lax.all_gather(axis_a, OBS, axis=0, tiled=True)
    kernel_a = lax.all_gather(kernel_a, LVL, axis=1, tiled=True)
    kernel_b = lax.all_gather(axis_b, LVL, axis=0, tiled=True)
    rows = jnp.arange(levels * grid_first, dtype=jnp.int32)
    collect = (rows[:, None] == places[None, :]).astype(jnp.bfloat16)
    pick = (places[:, None] == rows[None, :]).astype(jnp.bfloat16)

    def axis_pass(field):
        first = jnp.einsum(
            "larb,lbc->larc", field, kernel_b, preferred_element_type=jnp.float32
        ).astype(jnp.bfloat16)
        return jnp.einsum(
            "xla,larc->lxrc", kernel_a, first, preferred_element_type=jnp.float32
        ).astype(jnp.bfloat16)

    def operator(direction):
        low = direction.astype(jnp.bfloat16).reshape(columns, tile_count, tile_obs)
        part = jnp.einsum(
            "ctk,tkn->ctn", low, tile_weights, preferred_element_type=jnp.float32
        ).astype(jnp.bfloat16)
        part = part.reshape(chips, per_chip, tile_count, node_cols)
        part = lax.all_to_all(part, CHIPS, split_axis=0, concat_axis=0, tiled=True)
        part = jnp.swapaxes(part, 1, 2).reshape(chips * tile_count, per_chip * node_cols)
        summed = jnp.dot(collect, part, preferred_element_type=jnp.float32)
        summed = lax.psum(summed, CORE).astype(jnp.bfloat16)
        spread = axis_pass(summed.reshape(levels, grid_first, per_chip, node_cols))
        mixed = jnp.einsum(
            "lm,marc->larc",
            coupling,
            spread.astype(jnp.float32),
            precision=lax.Precision.HIGHEST,
        ).astype(jnp.bfloat16)
        values = axis_pass(mixed).reshape(levels * grid_first, per_chip * node_cols)
        back = jnp.dot(pick, values, preferred_element_type=jnp.float32).astype(jnp.bfloat16)
        back = back.reshape(chips, tile_count, per_chip, node_cols)
        back = jnp.swapaxes(back, 1, 2)
        back = lax.all_to_all(back, CHIPS, split_axis=0, concat_axis=0, tiled=True)
        back = back.reshape(columns, tile_count, node_cols)
        back = jnp.einsum(
            "ctn,tkn->ctk", back, tile_weights, preferred_element_type=jnp.float32
        ).astype(jnp.bfloat16)
        back = back.reshape(columns, tile_count * tile_obs)
        return back.astype(jnp.float32) + noise[:, None] * direction

    def total(field):
        return lax.psum(jnp.sum(field, axis=1), OBS_LVL)

    solution = jnp.zeros_like(rhs)
    residual = rhs
    direction = rhs
    norm_now = total(residual * residual)
    for step in range(ITERS):
        image = operator(direction)
        alpha = norm_now / total(direction * image)
        solution = solution + alpha[:, None] * direction
        residual = residual - alpha[:, None] * image
        if step + 1 < ITERS:
            norm_next = total(residual * residual)
            direction = residual + (norm_next / norm_now)[:, None] * direction
            norm_now = norm_next
    return (solution, residual)


def solution(mesh):
    split = Mesh(mesh.devices.reshape(4, 4, 4, 2), OBS_LVL)
    in_specs = (
        P(None, OBS_LVL),
        P(OBS_LVL, None, None),
        P(OBS_LVL, None),
        P(OBS_LVL),
        P(OBS, LVL, None),
        P(LVL, None, None),
        P(),
        P(),
    )
    out_specs = (P(None, OBS_LVL), P(None, OBS_LVL))
    return jax.shard_map(
        on_device, mesh=split, in_specs=in_specs, out_specs=out_specs, check_vma=False
    )
```

```python
import functools

import jax
import jax.numpy as jnp
from jax import lax
from jax.experimental import pallas as pl
from jax.experimental.pallas import tpu as pltpu
from jax.sharding import Mesh
from jax.sharding import PartitionSpec as P

AXES = ("obs_0", "obs_1", "lvl_0", "lvl_1")
OBS = ("obs_0", "obs_1")
LVL = ("lvl_0", "lvl_1")
MESH = pl.DeviceIdType.MESH

SIDE = 4
CHIPS = SIDE**3
LEVELS = 8
GRID_A = 128
NODES = 128
TILES = 128
TILE_OBS = 64
GROUP = 4
GROUPS = CHIPS // GROUP
QUAD = 4
WIDTH = QUAD * TILE_OBS
PITCH = TILES + 8
F32 = jnp.float32
BF16 = jnp.bfloat16


def dot(a, b):
    return jnp.dot(a, b, preferred_element_type=F32)


def two(v):
    return jnp.concatenate([v, v], axis=1)


def kernel(
    rhs_hbm,
    weights_hbm,
    place_ref,
    axis_a_ref,
    axis_b_ref,
    coupling_ref,
    noise_ref,
    noise_rows_ref,
    solution_ref,
    residual_ref,
    rhs_ref,
    weights_ref,
    turn,
    out_buf,
    in_buf,
    ret_buf,
    got_buf,
    places,
    spread_places,
    all_a,
    all_b,
    mat_a,
    acc,
    first_sums,
    partner_acc,
    grid_values,
    passed,
    stat_out,
    stat_in,
    stat_sum,
    stat_partner,
    coef_out,
    coef_in,
    coef_rows,
    load_sem,
    out_sem,
    in_sem,
    ret_sem,
    got_sem,
    place_sem,
    a_sem,
    b_sem,
    ab_sem,
    small_send_sem,
    stat_sem,
    coef_sem,
    acc_send_sem,
    acc_sem,
    tot_send_sem,
    tot_sem,
):
    z, y, x, core = (lax.axis_index(a) for a in AXES)
    me = (z * SIDE + y) * SIDE + x

    def offset(k):
        low, mid, high = k % SIDE, (k // SIDE) % SIDE, k // (SIDE * SIDE)
        return high + mid + low, mid + 2 * low, low

    def ahead(k):
        dz, dy, dx = offset(k)
        return (z + dz) % SIDE, (y + dy) % SIDE, (x + dx) % SIDE

    def behind(k):
        dz, dy, dx = offset(k)
        return (z + 12 - dz) % SIDE, (y + 12 - dy) % SIDE, (x + 12 - dx) % SIDE

    def chip(place):
        return (place[0] * SIDE + place[1]) * SIDE + place[2]

    def remote(src, dst, send, recv, place):
        return pltpu.make_async_remote_copy(
            src, dst, send, recv, device_id=(*place, core), device_id_type=MESH
        )

    def to_partner(src, dst, send, recv):
        return pltpu.make_async_remote_copy(
            src, dst, send, recv, device_id=(z, y, x, 1 - core), device_id_type=MESH
        )

    def local(src, dst, sem):
        pltpu.make_async_copy(src, dst, sem).start()

    def done(ref, sem):
        pltpu.make_async_copy(ref, ref, sem).wait()

    def each(start, stop, body):
        def step(k, unused):
            body(k)
            return unused

        lax.fori_loop(start, stop, step, 0)

    loads = [
        pltpu.make_async_copy(rhs_hbm, rhs_ref, load_sem.at[0]),
        pltpu.make_async_copy(weights_hbm, weights_ref, load_sem.at[1]),
    ]
    for load in loads:
        load.start()
    barrier = pltpu.get_barrier_semaphore()

    @functools.partial(each, 1, CHIPS)
    def _(k):
        pl.semaphore_signal(
            barrier, inc=1, device_id=(*ahead(k), core), device_id_type=MESH
        )

    pl.semaphore_signal(
        barrier, inc=1, device_id=(z, y, x, 1 - core), device_id_type=MESH
    )
    for load in loads:
        load.wait()

    lane = lax.broadcasted_iota(jnp.int32, (CHIPS, WIDTH), 1)
    in_tile = [lane // TILE_OBS == q for q in range(QUAD)]
    half = lax.broadcasted_iota(jnp.int32, (CHIPS, NODES), 1) < TILE_OBS
    rows = lax.broadcasted_iota(jnp.int32, (LEVELS * GRID_A, TILES), 0).astype(F32)
    cols = lax.broadcasted_iota(jnp.int32, (GROUP * TILES, NODES), 1).astype(F32)
    rest = pl.ds(1, CHIPS - 1)

    def window(i):
        return pl.ds(pl.multiple_of(i * WIDTH, WIDTH), WIDTH)

    def column(c):
        return pl.ds(pl.multiple_of(c * PITCH, 8), TILES)

    def spread_out(i, values):
        low = jnp.concatenate(
            [jnp.where(m, values, 0.0).astype(BF16) for m in in_tile], axis=0
        )
        part = dot(low, weights_ref[window(i), :])
        for q in range(QUAD):
            turn[pl.ds(QUAD * i + q, CHIPS, stride=PITCH), :] = part[
                q * CHIPS : (q + 1) * CHIPS
            ]

    def gather_back(i):
        values = jnp.concatenate(
            [
                turn[pl.ds(QUAD * i + q, CHIPS, stride=PITCH), :].astype(BF16)
                for q in range(QUAD)
            ],
            axis=0,
        )
        full = lax.dot_general(
            values,
            weights_ref[window(i), :],
            (((1,), (1,)), ((), ())),
            preferred_element_type=F32,
        )
        parts = []
        for h in range(QUAD // 2):
            lanes = slice(h * NODES, (h + 1) * NODES)
            even = full[2 * h * CHIPS : (2 * h + 1) * CHIPS, lanes]
            odd = full[(2 * h + 1) * CHIPS : (2 * h + 2) * CHIPS, lanes]
            parts.append(jnp.where(half, even, odd))
        return jnp.concatenate(parts, axis=1)

    def folded(product):
        return product[:, :NODES] + product[:, NODES:]

    def stat_rows(index, sums):
        for c in range(CHIPS):
            stat_out[index, c, :, :] = sums[c : c + 1, :]

    def send_parts(stats):
        def pack(k):
            out_buf[k] = turn[column(chip(ahead(k))), :].astype(BF16)

        def copy(k):
            return remote(
                out_buf.at[k], in_buf.at[k], out_sem, in_sem.at[k // GROUP], ahead(k)
            )

        pack(0)
        pack(1)
        local(out_buf.at[0], in_buf.at[0], in_sem.at[0])

        @functools.partial(each, 2, CHIPS)
        def _(k):
            pack(k)
            copy(k - 1).start()

        copy(CHIPS - 1).start()
        for s in range(stats):
            local(stat_out.at[s, me], stat_in.at[s, 0], stat_sem.at[s])

            @functools.partial(each, 1, CHIPS)
            def _(k):
                remote(
                    stat_out.at[s, chip(ahead(k))],
                    stat_in.at[s, k],
                    small_send_sem.at[s],
                    stat_sem.at[s],
                    ahead(k),
                ).start()

    def collect_parts():
        acc[...] = jnp.zeros_like(acc)

        @functools.partial(each, 0, GROUPS)
        def _(g):
            slots = pl.ds(g * GROUP, GROUP)
            done(in_buf.at[slots], in_sem.at[g])
            chosen = jnp.concatenate(
                [
                    jnp.where(rows == places[g * GROUP + j], 1.0, 0.0).astype(BF16)
                    for j in range(GROUP)
                ],
                axis=1,
            )
            parts = in_buf[slots].reshape(GROUP * TILES, NODES)
            acc[...] += dot(chosen, parts).reshape(LEVELS, GRID_A, NODES)

    def exchange(step, stats):
        for s in range(stats):
            done(stat_in.at[s], stat_sem.at[s])
            stat_sum[step, s] = jnp.sum(stat_in[s], axis=0)
        copies = [
            to_partner(
                acc.at[l],
                partner_acc.at[step, l],
                acc_send_sem.at[step, l],
                acc_sem.at[step, l],
            )
            for l in range(LEVELS)
        ]
        for copy in copies:
            copy.start()
        total = to_partner(
            stat_sum.at[step], stat_partner.at[step], tot_send_sem.at[step], tot_sem.at[step]
        )
        total.start()
        return copies, total

    def axis_pass(l, field):
        first = dot(field.astype(BF16), all_b[l % 2, l // 2]).astype(BF16)
        return dot(mat_a[l], first)

    def grid_step(step, copies, beta):
        for l in range(LEVELS):
            copies[l].wait()
            sums = acc[l] + partner_acc[step, l]
            if step:
                sums = sums + beta * first_sums[l]
            first_sums[l] = sums
            passed[l] = axis_pass(l, sums).astype(BF16)
        product = jnp.zeros((8, NODES), F32)
        for l in range(LEVELS):
            mixed = jnp.zeros((GRID_A, NODES), F32)
            for m in range(LEVELS):
                mixed = mixed + coupling_ref[l, m] * passed[m].astype(F32)
            values = axis_pass(l, mixed).astype(BF16)
            grid_values[l * GRID_A : (l + 1) * GRID_A, :] = values
            terms = first_sums[l] * values.astype(F32)
            product = product + jnp.sum(terms.reshape(GRID_A // 8, 8, NODES), axis=0)
        return jnp.sum(product)

    def send_back():
        def copy(k):
            return remote(
                ret_buf.at[k], got_buf.at[me], ret_sem, got_sem.at[k // GROUP], behind(k)
            )

        def pick(g):
            slots = pl.ds(g * GROUP, GROUP)
            where = spread_places[slots].reshape(GROUP * TILES, NODES)
            chosen = jnp.concatenate(
                [
                    jnp.where(where == cols + float(l * NODES), 1.0, 0.0).astype(BF16)
                    for l in range(LEVELS)
                ],
                axis=1,
            )
            ret_buf[slots] = (
                dot(chosen, grid_values[...]).astype(BF16).reshape(GROUP, TILES, NODES)
            )

        pick(0)
        pick(1)
        local(ret_buf.at[0], got_buf.at[me], got_sem.at[0])
        for k in range(1, GROUP):
            copy(k).start()

        @functools.partial(each, 2, GROUPS)
        def _(g):
            pick(g)
            for j in range(GROUP):
                copy((g - 1) * GROUP + j).start()

        for j in range(GROUP):
            copy((GROUPS - 1) * GROUP + j).start()

    def send_coefs(slot):
        local(coef_out.at[slot], coef_in.at[slot, me], coef_sem.at[slot])

        @functools.partial(each, 1, CHIPS)
        def _(k):
            remote(
                coef_out.at[slot],
                coef_in.at[slot, me],
                small_send_sem.at[2 + slot],
                coef_sem.at[slot],
                behind(k),
            ).start()

    def receive_coefs(slot):
        done(coef_in.at[slot], coef_sem.at[slot])
        for c in range(CHIPS):
            coef_rows[slot, c : c + 1, :] = coef_in[slot, c]

    def receive_back():
        @functools.partial(each, 0, GROUPS)
        def _(g):
            done(got_buf.at[pl.ds(g * GROUP, GROUP)], got_sem.at[g])
            for j in range(GROUP):
                c = chip(ahead(g * GROUP + j))
                turn[column(c), :] = got_buf[c].astype(F32)

    def rhs_quad(i, total):
        values = rhs_ref[:, window(i)]
        spread_out(i, values)
        return total + folded(values * values)

    zero = jnp.zeros((CHIPS, NODES), F32)
    total = lax.fori_loop(0, TILES // QUAD, rhs_quad, zero)
    stat_rows(0, total)

    pl.semaphore_wait(barrier, CHIPS)
    own_obs = z * SIDE + y
    local(place_ref, places.at[0], place_sem)
    local(axis_a_ref, all_a.at[core, x, own_obs], a_sem)
    local(axis_b_ref, all_b.at[core, x], b_sem)

    @functools.partial(each, 1, CHIPS)
    def _(k):
        to = ahead(k)
        remote(place_ref, places.at[k], small_send_sem.at[5], place_sem, to).start()
        remote(
            axis_a_ref, all_a.at[core, x, own_obs], small_send_sem.at[6], a_sem, to
        ).start()

    for d in range(1, SIDE):
        remote(
            axis_b_ref,
            all_b.at[core, x],
            small_send_sem.at[7],
            b_sem,
            (z, y, (x + d) % SIDE),
        ).start()
    send_parts(1)

    done(places, place_sem)

    @functools.partial(each, 0, CHIPS)
    def _(k):
        spread_places[k] = jnp.transpose(jnp.broadcast_to(places[k], (TILES, NODES)))

    done(all_a.at[core], a_sem)
    done(all_b.at[core], b_sem)
    shared = [
        to_partner(all_a.at[core], all_a.at[core], small_send_sem.at[8], ab_sem.at[0]),
        to_partner(all_b.at[core], all_b.at[core], small_send_sem.at[9], ab_sem.at[1]),
    ]
    for copy in shared:
        copy.start()
    for copy in shared:
        copy.wait()
    for l in range(LEVELS):
        mat_a[l] = all_a[l % 2, l // 2].astype(F32).reshape(GRID_A, GRID_A).astype(BF16)

    collect_parts()
    copies, total = exchange(0, 1)
    product = grid_step(0, copies, None)
    send_back()
    total.wait()
    norm_first = jnp.sum(stat_sum[0, 0] + stat_partner[0, 0])
    my_noise = noise_ref[me]
    coef_out[0] = jnp.full((1, NODES), norm_first) / jnp.full(
        (1, NODES), product + my_noise * norm_first
    )
    send_coefs(0)

    receive_back()
    receive_coefs(0)
    done(out_buf.at[rest], out_sem)
    done(stat_out.at[0, rest], small_send_sem.at[0])

    def residual_quad(i, carry):
        total, cross = carry
        start = rhs_ref[:, window(i)]
        image = gather_back(i) + two(noise_rows_ref[...]) * start
        values = start - two(coef_rows[0]) * image
        residual_ref[:, window(i)] = values
        spread_out(i, values)
        return total + folded(values * values), cross + folded(values * start)

    total, cross = lax.fori_loop(0, TILES // QUAD, residual_quad, (zero, zero))
    stat_rows(0, total)
    stat_rows(1, cross)
    send_parts(2)
    collect_parts()
    copies, total = exchange(1, 2)
    total.wait()
    norm_next = jnp.sum(stat_sum[1, 0] + stat_partner[1, 0])
    crossed = jnp.sum(stat_sum[1, 1] + stat_partner[1, 1])
    beta = jnp.full((1, NODES), norm_next) / jnp.full((1, NODES), norm_first)
    done(ret_buf.at[rest], ret_sem)
    coef_out[1] = beta
    product = grid_step(1, copies, beta)
    send_back()
    length = norm_next + 2.0 * beta * crossed + beta * beta * norm_first
    coef_out[2] = jnp.full((1, NODES), norm_next) / (product + my_noise * length)
    send_coefs(1)
    send_coefs(2)

    receive_back()
    receive_coefs(1)
    receive_coefs(2)

    def final_quad(i, unused):
        start = rhs_ref[:, window(i)]
        left = residual_ref[:, window(i)]
        direction = left + two(coef_rows[1]) * start
        image = gather_back(i) + two(noise_rows_ref[...]) * direction
        alpha = two(coef_rows[2])
        solution_ref[:, window(i)] = two(coef_rows[0]) * start + alpha * direction
        residual_ref[:, window(i)] = left - alpha * image
        return unused

    lax.fori_loop(0, TILES // QUAD, final_quad, 0)

    done(out_buf.at[rest], out_sem)
    done(ret_buf.at[rest], ret_sem)
    for s in range(2):
        done(stat_out.at[s, rest], small_send_sem.at[s])
    for slot in range(3):
        done(coef_in.at[slot, rest], small_send_sem.at[2 + slot])
    done(places.at[rest], small_send_sem.at[5])
    done(turn.at[pl.ds(0, (CHIPS - 1) * 4)], small_send_sem.at[6])
    done(all_b.at[0, pl.ds(1, SIDE - 1)], small_send_sem.at[7])


def on_device(rhs, tile_weights, tile_owner, tile_row, axis_a, axis_b, coupling, noise):
    lvl_count = lax.axis_size(LVL)
    tile_count, tile_obs, node_cols = tile_weights.shape
    columns, width = rhs.shape
    a_rows, lvl_here, grid_first = axis_a.shape
    owner = tile_owner[:, 0]
    level = (owner % lvl_count) * lvl_here + tile_row % lvl_here
    first_index = owner // lvl_count * a_rows + tile_row // lvl_here
    place = (level * grid_first + first_index).astype(F32).reshape(1, tile_count)
    anywhere = pl.BlockSpec(memory_space=pl.ANY)
    vmem = pl.BlockSpec(memory_space=pltpu.VMEM)
    smem = pl.BlockSpec(memory_space=pltpu.SMEM)
    dma = pltpu.SemaphoreType.DMA
    whole = jax.ShapeDtypeStruct((columns, width), F32)
    slots = (CHIPS, TILES, NODES)
    return pl.pallas_call(
        kernel,
        out_shape=(whole, whole),
        in_specs=[anywhere, anywhere, vmem, vmem, vmem, smem, smem, vmem],
        out_specs=(vmem, vmem),
        scratch_shapes=[
            pltpu.VMEM((columns, width), F32),
            pltpu.VMEM((tile_count * tile_obs, node_cols), BF16),
            pltpu.VMEM((CHIPS * PITCH, NODES), F32),
            pltpu.VMEM(slots, BF16),
            pltpu.VMEM(slots, BF16),
            pltpu.VMEM(slots, BF16),
            pltpu.VMEM(slots, BF16),
            pltpu.VMEM((CHIPS, 1, TILES), F32),
            pltpu.VMEM(slots, F32),
            pltpu.VMEM((2, SIDE, SIDE * SIDE, a_rows, grid_first), BF16),
            pltpu.VMEM((2, SIDE, NODES, NODES), BF16),
            pltpu.VMEM((LEVELS, GRID_A, GRID_A), BF16),
            pltpu.VMEM((LEVELS, GRID_A, NODES), F32),
            pltpu.VMEM((LEVELS, GRID_A, NODES), F32),
            pltpu.VMEM((2, LEVELS, GRID_A, NODES), F32),
            pltpu.VMEM((LEVELS * GRID_A, NODES), BF16),
            pltpu.VMEM((LEVELS, GRID_A, NODES), BF16),
            pltpu.VMEM((2, CHIPS, 1, NODES), F32),
            pltpu.VMEM((2, CHIPS, 1, NODES), F32),
            pltpu.VMEM((2, 2, 1, NODES), F32),
            pltpu.VMEM((2, 2, 1, NODES), F32),
            pltpu.VMEM((3, 1, NODES), F32),
            pltpu.VMEM((3, CHIPS, 1, NODES), F32),
            pltpu.VMEM((3, CHIPS, NODES), F32),
            dma((2,)),
            dma,
            dma((GROUPS,)),
            dma,
            dma((GROUPS,)),
            dma,
            dma,
            dma,
            dma((2,)),
            dma((10,)),
            dma((2,)),
            dma((3,)),
            dma((2, LEVELS)),
            dma((2, LEVELS)),
            dma((2,)),
            dma((2,)),
        ],
        compiler_params=pltpu.CompilerParams(
            collective_id=0, has_side_effects=True, vmem_limit_bytes=60 << 20
        ),
        name="conjugate_gradients",
    )(
        rhs,
        tile_weights.reshape(tile_count * tile_obs, node_cols),
        place,
        axis_a.reshape(a_rows, grid_first),
        axis_b.reshape(node_cols, node_cols),
        coupling,
        noise,
        jnp.broadcast_to(noise[:, None], (columns, NODES)),
    )


def solution(mesh):
    split = Mesh(mesh.devices.reshape(SIDE, SIDE, SIDE, 2), AXES)
    in_specs = (
        P(None, AXES),
        P(AXES, None, None),
        P(AXES, None),
        P(AXES),
        P(OBS, LVL, None),
        P(LVL, None, None),
        P(),
        P(),
    )
    out_specs = (P(None, AXES), P(None, AXES))
    return jax.shard_map(
        on_device, mesh=split, in_specs=in_specs, out_specs=out_specs, check_vma=False
    )
```

```python
import functools

import jax
import jax.numpy as jnp
from jax import lax
from jax.experimental import pallas as pl
from jax.experimental.pallas import tpu as pltpu
from jax.sharding import Mesh
from jax.sharding import PartitionSpec as P

AXES = ("obs_0", "obs_1", "lvl_0", "lvl_1")
OBS = ("obs_0", "obs_1")
LVL = ("lvl_0", "lvl_1")
MESH = pl.DeviceIdType.MESH

SIDE = 4
CHIPS = SIDE**3
LEVELS = 8
GRID_A = 128
NODES = 128
TILES = 128
TILE_OBS = 64
PARTS = 2
PART = TILES // PARTS
GROUP = 8
GROUPS = CHIPS // GROUP
QUAD = 4
WIDTH = QUAD * TILE_OBS
PAIRS = PART // QUAD // 2
PITCH = TILES + 8
F32 = jnp.float32
BF16 = jnp.bfloat16


def dot(a, b):
    return jnp.dot(a, b, preferred_element_type=F32)


def two(v):
    return jnp.concatenate([v, v], axis=1)


def kernel(
    rhs_hbm,
    weights_hbm,
    owner_ref,
    row_ref,
    axis_a_ref,
    axis_b_ref,
    coupling_ref,
    noise_ref,
    solution_ref,
    residual_ref,
    rhs_ref,
    weights_ref,
    turn,
    out_buf,
    in_buf,
    ret_buf,
    got_buf,
    place_out,
    places,
    part_places,
    spread_places,
    all_a,
    all_b,
    mat_a,
    acc,
    node_sums,
    partner_acc,
    grid_values,
    passed,
    noise_rows,
    stat_out,
    stat_in,
    stat_sum,
    stat_partner,
    coef_out,
    coef_in,
    coef_rows,
    load_sem,
    out_sem,
    in_sem,
    ret_sem,
    got_sem,
    place_sem,
    a_sem,
    b_sem,
    ab_sem,
    small_sem,
    stat_sem,
    coef_sem,
    acc_send_sem,
    acc_sem,
    tot_send_sem,
    tot_sem,
):
    z, y, x, core = (lax.axis_index(a) for a in AXES)
    me = (z * SIDE + y) * SIDE + x
    mine = z * SIDE + y
    x_ahead = [lax.rem(x + d, SIDE) for d in range(SIDE)]
    x_behind = [lax.rem(x + SIDE - d, SIDE) for d in range(SIDE)]

    def ahead(q):
        places = []
        for j in range(GROUP):
            low, mid = j % SIDE, 2 * lax.rem(q, 2) + j // SIDE
            high = lax.div(q, 2)
            places.append(
                (
                    lax.rem(z + high + mid + low, SIDE),
                    lax.rem(y + mid + 2 * low, SIDE),
                    x_ahead[low],
                )
            )
        return places

    def behind(q):
        places = []
        for j in range(GROUP):
            low, mid = j % SIDE, 2 * lax.rem(q, 2) + j // SIDE
            high = lax.div(q, 2)
            places.append(
                (
                    lax.rem(z + 12 - (high + mid + low), SIDE),
                    lax.rem(y + 12 - (mid + 2 * low), SIDE),
                    x_behind[low],
                )
            )
        return places

    def chip(place):
        return (place[0] * SIDE + place[1]) * SIDE + place[2]

    def remote(src, dst, send, recv, place):
        return pltpu.make_async_remote_copy(
            src, dst, send, recv, device_id=(*place, core), device_id_type=MESH
        )

    def to_partner(src, dst, send, recv):
        return pltpu.make_async_remote_copy(
            src, dst, send, recv, device_id=(z, y, x, 1 - core), device_id_type=MESH
        )

    def local(src, dst, sem):
        pltpu.make_async_copy(src, dst, sem).start()

    def done(ref, sem):
        pltpu.make_async_copy(ref, ref, sem).wait()

    def each(start, stop, body):
        def step(k, unused):
            body(k)
            return unused

        lax.fori_loop(start, stop, step, 0)

    def others(places_of, body):
        def group(q, first):
            places = places_of(q)
            for j in range(first, GROUP):
                body(q * GROUP + j, places[j])

        group(0, 1)
        each(1, GROUPS, lambda q: group(q, 0))

    loads = []
    for h in range(PARTS):
        obs = pl.ds(h * PART * TILE_OBS, PART * TILE_OBS)
        loads.append(
            (
                pltpu.make_async_copy(rhs_hbm.at[:, obs], rhs_ref.at[:, obs], load_sem.at[0, h]),
                pltpu.make_async_copy(
                    weights_hbm.at[obs], weights_ref.at[obs], load_sem.at[1, h]
                ),
            )
        )
        for load in loads[h]:
            load.start()
    barrier = pltpu.get_barrier_semaphore()

    def greet(place):
        pl.semaphore_signal(barrier, inc=1, device_id=place, device_id_type=MESH)

    others(ahead, lambda k, place: greet((*place, core)))
    greet((z, y, x, 1 - core))

    lane = lax.broadcasted_iota(jnp.int32, (CHIPS, WIDTH), 1)
    in_tile = [lane // TILE_OBS == q for q in range(QUAD)]
    half = lax.broadcasted_iota(jnp.int32, (CHIPS, NODES), 1) < TILE_OBS
    rows = lax.broadcasted_iota(jnp.int32, (LEVELS * GRID_A, NODES), 0).astype(F32)
    cols = lax.broadcasted_iota(jnp.int32, (GROUP * PART, NODES), 1).astype(F32)
    rest = pl.ds(1, CHIPS - 1)

    owner = owner_ref[...]
    base = (owner & (LEVELS - 1)) * GRID_A + (owner >> 3) * (GRID_A // 16)
    base = jnp.transpose(jnp.broadcast_to(base.astype(F32), (TILES, NODES)))
    place_out[...] = base[0:1, :] + row_ref[...].astype(F32)

    def window(i):
        return pl.ds(pl.multiple_of(i * WIDTH, WIDTH), WIDTH)

    def column(c, h):
        return pl.ds(pl.multiple_of(c * PITCH + h * PART, 8), PART)

    def tile(t):
        return pl.ds(t, CHIPS, stride=PITCH)

    def spread_out(quads, values):
        parts = []
        for i, v in zip(quads, values):
            low = jnp.concatenate(
                [jnp.where(m, v, 0.0).astype(BF16) for m in in_tile], axis=0
            )
            parts.append(dot(low, weights_ref[window(i), :]))
        for i, part in zip(quads, parts):
            for q in range(QUAD):
                turn[tile(QUAD * i + q), :] = part[q * CHIPS : (q + 1) * CHIPS]

    def gather_back(quads):
        fulls = []
        for i in quads:
            values = jnp.concatenate(
                [turn[tile(QUAD * i + q), :].astype(BF16) for q in range(QUAD)], axis=0
            )
            fulls.append(
                lax.dot_general(
                    values,
                    weights_ref[window(i), :],
                    (((1,), (1,)), ((), ())),
                    preferred_element_type=F32,
                )
            )
        out = []
        for full in fulls:
            parts = []
            for p in range(QUAD // 2):
                lanes = slice(p * NODES, (p + 1) * NODES)
                even = full[2 * p * CHIPS : (2 * p + 1) * CHIPS, lanes]
                odd = full[(2 * p + 1) * CHIPS : (2 * p + 2) * CHIPS, lanes]
                parts.append(jnp.where(half, even, odd))
            out.append(jnp.concatenate(parts, axis=1))
        return out

    def folded(product):
        return product[:, :NODES] + product[:, NODES:]

    def send_part(h):
        def pack(q):
            for j, place in enumerate(ahead(q)):
                out_buf[h, q * GROUP + j] = turn[column(chip(place), h), :].astype(BF16)

        def start(q, first=0):
            for j, place in list(enumerate(ahead(q)))[first:]:
                k = q * GROUP + j
                remote(
                    out_buf.at[h, k], in_buf.at[h, k], out_sem.at[h], in_sem.at[h, q], place
                ).start()

        pack(0)
        pack(1)
        local(out_buf.at[h, 0], in_buf.at[h, 0], in_sem.at[h, 0])
        start(0, 1)

        @functools.partial(each, 2, GROUPS)
        def _(q):
            pack(q)
            start(q - 1)

        start(GROUPS - 1)

    def send_stats(first, second):
        for c in range(CHIPS):
            stat_out[c, :, :NODES] = first[c : c + 1, :]
            stat_out[c, :, NODES:] = second[c : c + 1, :]
        local(stat_out.at[me], stat_in.at[0], stat_sem)
        others(
            ahead,
            lambda k, place: remote(
                stat_out.at[chip(place)], stat_in.at[k], small_sem.at[0], stat_sem, place
            ).start(),
        )

    def collect_part(h):
        per_row = NODES // PART
        group_rows = GROUP // per_row

        @functools.partial(each, 0, GROUPS)
        def _(q):
            slots = pl.ds(q * GROUP, GROUP)
            done(in_buf.at[h, slots], in_sem.at[h, q])
            chosen = jnp.concatenate(
                [
                    jnp.where(rows == part_places[h, q * group_rows + j], 1.0, 0.0).astype(BF16)
                    for j in range(group_rows)
                ],
                axis=1,
            )
            parts = in_buf[h, slots].reshape(GROUP * PART, NODES)
            acc[...] += dot(chosen, parts).reshape(LEVELS, GRID_A, NODES)

    def exchange(step):
        copies = [
            to_partner(
                acc.at[l],
                partner_acc.at[step, l],
                acc_send_sem.at[step, l],
                acc_sem.at[step, l],
            )
            for l in range(LEVELS)
        ]
        for copy in copies:
            copy.start()
        done(stat_in, stat_sem)
        stat_sum[step] = jnp.sum(stat_in[...], axis=0)
        total = to_partner(
            stat_sum.at[step], stat_partner.at[step], tot_send_sem.at[step], tot_sem.at[step]
        )
        total.start()
        return copies, total

    def axis_passes(fields):
        firsts = [
            dot(field.astype(BF16), all_b[l % 2, l // 2]).astype(BF16)
            for l, field in enumerate(fields)
        ]
        return [dot(mat_a[l], first).astype(BF16) for l, first in enumerate(firsts)]

    def grid_step(step, copies, beta):
        for copy in copies:
            copy.wait()
        fields = []
        for l in range(LEVELS):
            sums = acc[l] + partner_acc[step, l]
            if step:
                sums = sums + beta * node_sums[l]
            node_sums[l] = sums
            fields.append(sums)
        for l, spread in enumerate(axis_passes(fields)):
            passed[l] = spread
        fields = []
        for l in range(LEVELS):
            mixed = coupling_ref[l, 0] * passed[0].astype(F32)
            for m in range(1, LEVELS):
                mixed = mixed + coupling_ref[l, m] * passed[m].astype(F32)
            fields.append(mixed)
        for l, values in enumerate(axis_passes(fields)):
            grid_values[l * GRID_A : (l + 1) * GRID_A, :] = values

    def curvature():
        product = jnp.zeros((8, NODES), F32)
        for l in range(LEVELS):
            terms = node_sums[l] * grid_values[l * GRID_A : (l + 1) * GRID_A, :].astype(F32)
            product = product + jnp.sum(terms.reshape(GRID_A // 8, 8, NODES), axis=0)
        return jnp.sum(product)

    def send_back(h, between):
        def pick(q):
            slots = pl.ds(q * GROUP, GROUP)
            where = spread_places[slots, pl.ds(h * PART, PART)].reshape(GROUP * PART, NODES)
            chosen = jnp.concatenate(
                [
                    jnp.where(where == cols + float(l * NODES), 1.0, 0.0).astype(BF16)
                    for l in range(LEVELS)
                ],
                axis=1,
            )
            ret_buf[h, slots] = (
                dot(chosen, grid_values[...]).astype(BF16).reshape(GROUP, PART, NODES)
            )

        def start(q, first=0):
            for j, place in list(enumerate(behind(q)))[first:]:
                remote(
                    ret_buf.at[h, q * GROUP + j],
                    got_buf.at[h, me],
                    ret_sem.at[h],
                    got_sem.at[h, q],
                    place,
                ).start()

        pick(0)
        between()
        local(ret_buf.at[h, 0], got_buf.at[h, me], got_sem.at[h, 0])
        start(0, 1)
        pick(1)

        @functools.partial(each, 2, GROUPS)
        def _(q):
            start(q - 1)
            pick(q)

        start(GROUPS - 1)

    def send_coefs(step):
        local(coef_out.at[step], coef_in.at[step, me], coef_sem.at[step])
        others(
            behind,
            lambda k, place: remote(
                coef_out.at[step],
                coef_in.at[step, me],
                small_sem.at[1 + step],
                coef_sem.at[step],
                place,
            ).start(),
        )

    def receive_coefs(step):
        done(coef_in.at[step], coef_sem.at[step])
        for c in range(CHIPS):
            coef_rows[step, c : c + 1, :] = coef_in[step, c]

    def receive_part(h):
        @functools.partial(each, 0, GROUPS)
        def _(q):
            done(got_buf.at[h, pl.ds(q * GROUP, GROUP)], got_sem.at[h, q])
            for place in ahead(q):
                c = chip(place)
                turn[column(c, h), :] = got_buf[h, c].astype(F32)

    def over_part(h, body, carry):
        def step(p, carry):
            i = h * PAIRS * 2 + 2 * p
            return body((i, i + 1), carry)

        return lax.fori_loop(0, PAIRS, step, carry)

    def rhs_quads(quads, total):
        values = [rhs_ref[:, window(i)] for i in quads]
        spread_out(quads, values)
        for v in values:
            total = total + folded(v * v)
        return total

    zero = jnp.zeros((CHIPS, NODES), F32)
    total = zero
    for h in range(PARTS):
        for load in loads[h]:
            load.wait()
        total = over_part(h, rhs_quads, total)
        if h == 0:
            pl.semaphore_wait(barrier, CHIPS)
        send_part(h)
        if h == 0:
            local(place_out, places.at[0], place_sem)
            local(axis_a_ref, all_a.at[core, x, mine], a_sem)
            local(axis_b_ref, all_b.at[core, x], b_sem)

            def introduce(k, place):
                remote(place_out, places.at[k], small_sem.at[3], place_sem, place).start()
                remote(
                    axis_a_ref, all_a.at[core, x, mine], small_sem.at[4], a_sem, place
                ).start()

            others(ahead, introduce)
            for d in range(1, SIDE):
                remote(
                    axis_b_ref, all_b.at[core, x], small_sem.at[5], b_sem, (z, y, x_ahead[d])
                ).start()
    send_stats(total, total)

    for c in range(CHIPS):
        noise_rows[c : c + 1, :] = jnp.full((1, NODES), noise_ref[c])
    acc[...] = jnp.zeros_like(acc)
    done(places, place_sem)

    @functools.partial(each, 0, CHIPS)
    def _(k):
        spread_places[k] = jnp.transpose(jnp.broadcast_to(places[k], (TILES, NODES)))

    first_half = lax.broadcasted_iota(jnp.int32, (1, NODES), 1) < PART

    @functools.partial(each, 0, CHIPS // 2)
    def _(r):
        even, odd = places[2 * r], places[2 * r + 1]
        part_places[0, r] = jnp.where(first_half, even, pltpu.roll(odd, PART, 1))
        part_places[1, r] = jnp.where(first_half, pltpu.roll(even, PART, 1), odd)

    done(all_a.at[core], a_sem)
    done(all_b.at[core], b_sem)
    shared = [
        to_partner(all_a.at[core], all_a.at[core], small_sem.at[6], ab_sem.at[0]),
        to_partner(all_b.at[core], all_b.at[core], small_sem.at[7], ab_sem.at[1]),
    ]
    for copy in shared:
        copy.start()
    collect_part(0)
    for copy in shared:
        copy.wait()
    for l in range(LEVELS):
        mat_a[l] = all_a[l % 2, l // 2].astype(F32).reshape(GRID_A, GRID_A).astype(BF16)
    for h in range(1, PARTS):
        collect_part(h)
    copies, total = exchange(0)
    grid_step(0, copies, None)
    total.wait()
    norm_first = jnp.sum((stat_sum[0] + stat_partner[0])[:, :NODES])
    my_noise = noise_ref[me]

    def first_coefs():
        alpha = jnp.full((1, NODES), norm_first) / jnp.full(
            (1, NODES), curvature() + my_noise * norm_first
        )
        coef_out[0] = two(alpha)

    send_back(0, first_coefs)
    send_coefs(0)
    for h in range(1, PARTS):
        send_back(h, lambda: None)

    def residual_quads(quads, carry):
        total, cross = carry
        backs = gather_back(quads)
        values = []
        for i, back in zip(quads, backs):
            start = rhs_ref[:, window(i)]
            image = back + two(noise_rows[...]) * start
            v = start - coef_rows[0] * image
            residual_ref[:, window(i)] = v
            total = total + folded(v * v)
            cross = cross + folded(v * start)
            values.append(v)
        spread_out(quads, values)
        return total, cross

    acc[...] = jnp.zeros_like(acc)
    carry = (zero, zero)
    for h in range(PARTS):
        receive_part(h)
        if h == 0:
            receive_coefs(0)
        carry = over_part(h, residual_quads, carry)
        done(out_buf.at[h, rest], out_sem.at[h])
        send_part(h)
    done(stat_out.at[rest], small_sem.at[0])
    send_stats(*carry)
    for h in range(PARTS):
        collect_part(h)
    copies, total = exchange(1)
    total.wait()
    stats = stat_sum[1] + stat_partner[1]
    norm_next = jnp.sum(stats[:, :NODES])
    crossed = jnp.sum(stats[:, NODES:])
    beta = jnp.full((1, NODES), norm_next) / jnp.full((1, NODES), norm_first)
    grid_step(1, copies, beta)

    def second_coefs():
        length = norm_next + 2.0 * beta * crossed + beta * beta * norm_first
        alpha = jnp.full((1, NODES), norm_next) / (curvature() + my_noise * length)
        coef_out[1] = jnp.concatenate([alpha, beta], axis=1)

    for h in range(PARTS):
        done(ret_buf.at[h, rest], ret_sem.at[h])
    send_back(0, second_coefs)
    send_coefs(1)
    for h in range(1, PARTS):
        send_back(h, lambda: None)

    def final_quads(quads, carry):
        backs = gather_back(quads)
        alpha, beta = two(coef_rows[1, :, :NODES]), two(coef_rows[1, :, NODES:])
        for i, back in zip(quads, backs):
            start = rhs_ref[:, window(i)]
            left = residual_ref[:, window(i)]
            direction = left + beta * start
            image = back + two(noise_rows[...]) * direction
            solution_ref[:, window(i)] = coef_rows[0] * start + alpha * direction
            residual_ref[:, window(i)] = left - alpha * image
        return carry

    for h in range(PARTS):
        receive_part(h)
        if h == 0:
            receive_coefs(1)
        over_part(h, final_quads, 0)

    for h in range(PARTS):
        done(out_buf.at[h, rest], out_sem.at[h])
        done(ret_buf.at[h, rest], ret_sem.at[h])
    done(stat_out.at[rest], small_sem.at[0])
    for step in range(2):
        done(coef_in.at[step, rest], small_sem.at[1 + step])
    done(places.at[rest], small_sem.at[3])
    done(turn.at[pl.ds(0, (CHIPS - 1) * 4)], small_sem.at[4])
    done(all_b.at[0, pl.ds(1, SIDE - 1)], small_sem.at[5])


def on_device(rhs, tile_weights, tile_owner, tile_row, axis_a, axis_b, coupling, noise):
    tile_count, tile_obs, node_cols = tile_weights.shape
    columns, width = rhs.shape
    a_rows, lvl_here, grid_first = axis_a.shape
    anywhere = pl.BlockSpec(memory_space=pl.ANY)
    vmem = pl.BlockSpec(memory_space=pltpu.VMEM)
    smem = pl.BlockSpec(memory_space=pltpu.SMEM)
    dma = pltpu.SemaphoreType.DMA
    whole = pltpu.VMEM((columns, width), F32)
    parts = pltpu.VMEM((PARTS, CHIPS, PART, NODES), BF16)
    field = pltpu.VMEM((LEVELS, GRID_A, NODES), F32)
    return pl.pallas_call(
        kernel,
        out_shape=[jax.ShapeDtypeStruct((columns, width), F32)] * 2,
        in_specs=[anywhere, anywhere, vmem, vmem, vmem, vmem, smem, smem],
        out_specs=(vmem, vmem),
        scratch_shapes=[
            whole,
            pltpu.VMEM((tile_count * tile_obs, node_cols), BF16),
            pltpu.VMEM((CHIPS * PITCH, NODES), F32),
            parts,
            parts,
            parts,
            parts,
            pltpu.VMEM((1, TILES), F32),
            pltpu.VMEM((CHIPS, 1, TILES), F32),
            pltpu.VMEM((PARTS, CHIPS // 2, 1, NODES), F32),
            pltpu.VMEM((CHIPS, TILES, NODES), F32),
            pltpu.VMEM((2, SIDE, SIDE * SIDE, a_rows, grid_first), BF16),
            pltpu.VMEM((2, SIDE, NODES, NODES), BF16),
            pltpu.VMEM((LEVELS, GRID_A, GRID_A), BF16),
            field,
            field,
            pltpu.VMEM((2, LEVELS, GRID_A, NODES), F32),
            pltpu.VMEM((LEVELS * GRID_A, NODES), BF16),
            pltpu.VMEM((LEVELS, GRID_A, NODES), BF16),
            pltpu.VMEM((CHIPS, NODES), F32),
            pltpu.VMEM((CHIPS, 1, 2 * NODES), F32),
            pltpu.VMEM((CHIPS, 1, 2 * NODES), F32),
            pltpu.VMEM((2, 1, 2 * NODES), F32),
            pltpu.VMEM((2, 1, 2 * NODES), F32),
            pltpu.VMEM((2, 1, 2 * NODES), F32),
            pltpu.VMEM((2, CHIPS, 1, 2 * NODES), F32),
            pltpu.VMEM((2, CHIPS, 2 * NODES), F32),
            dma((2, PARTS)),
            dma((PARTS,)),
            dma((PARTS, GROUPS)),
            dma((PARTS,)),
            dma((PARTS, GROUPS)),
            dma,
            dma,
            dma,
            dma((2,)),
            dma((8,)),
            dma,
            dma((2,)),
            dma((2, LEVELS)),
            dma((2, LEVELS)),
            dma((2,)),
            dma((2,)),
        ],
        compiler_params=pltpu.CompilerParams(
            collective_id=0, has_side_effects=True, vmem_limit_bytes=60 << 20
        ),
        name="conjugate_gradients",
    )(
        rhs,
        tile_weights.reshape(tile_count * tile_obs, node_cols),
        tile_owner,
        tile_row.reshape(1, tile_count),
        axis_a.reshape(a_rows, grid_first),
        axis_b.reshape(node_cols, node_cols),
        coupling,
        noise,
    )


def solution(mesh):
    split = Mesh(mesh.devices.reshape(SIDE, SIDE, SIDE, 2), AXES)
    in_specs = (
        P(None, AXES),
        P(AXES, None, None),
        P(AXES, None),
        P(AXES),
        P(OBS, LVL, None),
        P(LVL, None, None),
        P(),
        P(),
    )
    out_specs = (P(None, AXES), P(None, AXES))
    return jax.shard_map(
        on_device, mesh=split, in_specs=in_specs, out_specs=out_specs, check_vma=False
    )
```

```python
import functools

import jax
import jax.numpy as jnp
from jax import lax
from jax.experimental import pallas as pl
from jax.experimental.pallas import tpu as pltpu
from jax.sharding import Mesh
from jax.sharding import PartitionSpec as P

AXES = ("obs_0", "obs_1", "lvl_0", "lvl_1")
OBS = ("obs_0", "obs_1")
LVL = ("lvl_0", "lvl_1")
MESH = pl.DeviceIdType.MESH

SIDE = 4
CHIPS = SIDE**3
LEVELS = 8
GRID_A = 128
NODES = 128
TILES = 128
TILE_OBS = 64
PARTS = 2
PART = TILES // PARTS
GROUP = 8
GROUPS = CHIPS // GROUP
QUAD = 4
WIDTH = QUAD * TILE_OBS
PAIRS = PART // QUAD // 2
PITCH = TILES + 8
F32 = jnp.float32
BF16 = jnp.bfloat16


def dot(a, b):
    return jnp.dot(a, b, preferred_element_type=F32)


def two(v):
    return jnp.concatenate([v, v], axis=1)


def kernel(
    rhs_hbm,
    weights_hbm,
    owner_ref,
    row_ref,
    axis_a_ref,
    axis_b_ref,
    coupling_ref,
    noise_ref,
    solution_ref,
    residual_ref,
    rhs_ref,
    weights_ref,
    turn,
    out_buf,
    in_buf,
    ret_buf,
    got_buf,
    place_out,
    places,
    part_places,
    spread_places,
    all_a,
    all_b,
    mat_a,
    acc,
    node_sums,
    partner_acc,
    grid_values,
    passed,
    noise_rows,
    stat_out,
    stat_in,
    stat_sum,
    stat_partner,
    coef_out,
    coef_in,
    coef_rows,
    load_sem,
    out_sem,
    in_sem,
    ret_sem,
    got_sem,
    place_sem,
    a_sem,
    b_sem,
    ab_sem,
    small_sem,
    stat_sem,
    coef_sem,
    acc_send_sem,
    acc_sem,
    tot_send_sem,
    tot_sem,
):
    z, y, x, core = (lax.axis_index(a) for a in AXES)
    me = (z * SIDE + y) * SIDE + x
    mine = z * SIDE + y
    way = 1 - 2 * core
    x_ahead = [lax.rem(x + SIDE + way * d, SIDE) for d in range(SIDE)]
    x_behind = [lax.rem(x + SIDE - way * d, SIDE) for d in range(SIDE)]

    def ahead(q):
        places = []
        for j in range(GROUP):
            low, mid = j % SIDE, 2 * lax.rem(q, 2) + j // SIDE
            high = lax.div(q, 2)
            places.append(
                (
                    lax.rem(z + 12 + way * (high + mid + low), SIDE),
                    lax.rem(y + 12 + way * (mid + 2 * low), SIDE),
                    x_ahead[low],
                )
            )
        return places

    def behind(q):
        places = []
        for j in range(GROUP):
            low, mid = j % SIDE, 2 * lax.rem(q, 2) + j // SIDE
            high = lax.div(q, 2)
            places.append(
                (
                    lax.rem(z + 12 - way * (high + mid + low), SIDE),
                    lax.rem(y + 12 - way * (mid + 2 * low), SIDE),
                    x_behind[low],
                )
            )
        return places

    def chip(place):
        return (place[0] * SIDE + place[1]) * SIDE + place[2]

    def remote(src, dst, send, recv, place):
        return pltpu.make_async_remote_copy(
            src, dst, send, recv, device_id=(*place, core), device_id_type=MESH
        )

    def to_partner(src, dst, send, recv):
        return pltpu.make_async_remote_copy(
            src, dst, send, recv, device_id=(z, y, x, 1 - core), device_id_type=MESH
        )

    def local(src, dst, sem):
        pltpu.make_async_copy(src, dst, sem).start()

    def done(ref, sem):
        pltpu.make_async_copy(ref, ref, sem).wait()

    def each(start, stop, body):
        def step(k, unused):
            body(k)
            return unused

        lax.fori_loop(start, stop, step, 0)

    def others(places_of, body):
        def group(q, first):
            places = places_of(q)
            for j in range(first, GROUP):
                body(q * GROUP + j, places[j])

        group(0, 1)
        each(1, GROUPS, lambda q: group(q, 0))

    loads = []
    for h in range(PARTS):
        obs = pl.ds(h * PART * TILE_OBS, PART * TILE_OBS)
        loads.append(
            (
                pltpu.make_async_copy(rhs_hbm.at[:, obs], rhs_ref.at[:, obs], load_sem.at[0, h]),
                pltpu.make_async_copy(
                    weights_hbm.at[obs], weights_ref.at[obs], load_sem.at[1, h]
                ),
            )
        )
        for load in loads[h]:
            load.start()
    barrier = pltpu.get_barrier_semaphore()

    def greet(place):
        pl.semaphore_signal(barrier, inc=1, device_id=place, device_id_type=MESH)

    around = [[lax.rem(v + d, SIDE) for d in range(SIDE)] for v in (z, y, x)]
    for k in range(CHIPS - 1, 0, -1):
        dz, dy, dx = k // (SIDE * SIDE), k // SIDE % SIDE, k % SIDE
        greet((around[0][dz], around[1][dy], around[2][dx], core))
    greet((z, y, x, 1 - core))

    lane = lax.broadcasted_iota(jnp.int32, (CHIPS, WIDTH), 1)
    in_tile = [lane // TILE_OBS == q for q in range(QUAD)]
    half = lax.broadcasted_iota(jnp.int32, (CHIPS, NODES), 1) < TILE_OBS
    rows = lax.broadcasted_iota(jnp.int32, (LEVELS * GRID_A, NODES), 0).astype(F32)
    cols = lax.broadcasted_iota(jnp.int32, (GROUP * PART, NODES), 1).astype(F32)
    rest = pl.ds(1, CHIPS - 1)

    owner = owner_ref[...]
    base = (owner & (LEVELS - 1)) * GRID_A + (owner >> 3) * (GRID_A // 16)
    place_out[...] = (base + row_ref[...]).astype(F32)

    def window(i):
        return pl.ds(pl.multiple_of(i * WIDTH, WIDTH), WIDTH)

    def column(c, h):
        return pl.ds(pl.multiple_of(c * PITCH + h * PART, 8), PART)

    def tile(t):
        return pl.ds(t, CHIPS, stride=PITCH)

    def spread_out(quads, values):
        parts = []
        for i, v in zip(quads, values):
            low = jnp.concatenate(
                [jnp.where(m, v, 0.0).astype(BF16) for m in in_tile], axis=0
            )
            parts.append(dot(low, weights_ref[window(i), :]))
        for i, part in zip(quads, parts):
            for q in range(QUAD):
                turn[tile(QUAD * i + q), :] = part[q * CHIPS : (q + 1) * CHIPS]

    def gather_back(quads):
        fulls = []
        for i in quads:
            values = jnp.concatenate(
                [turn[tile(QUAD * i + q), :].astype(BF16) for q in range(QUAD)], axis=0
            )
            fulls.append(
                lax.dot_general(
                    values,
                    weights_ref[window(i), :],
                    (((1,), (1,)), ((), ())),
                    preferred_element_type=F32,
                )
            )
        out = []
        for full in fulls:
            parts = []
            for p in range(QUAD // 2):
                lanes = slice(p * NODES, (p + 1) * NODES)
                even = full[2 * p * CHIPS : (2 * p + 1) * CHIPS, lanes]
                odd = full[(2 * p + 1) * CHIPS : (2 * p + 2) * CHIPS, lanes]
                parts.append(jnp.where(half, even, odd))
            out.append(jnp.concatenate(parts, axis=1))
        return out

    def folded(product):
        return product[:, :NODES] + product[:, NODES:]

    def send_part(h, between=lambda: None):
        def pack(q):
            for j, place in enumerate(ahead(q)):
                out_buf[h, q * GROUP + j] = turn[column(chip(place), h), :].astype(BF16)

        def start(q, first=0):
            for j, place in list(enumerate(ahead(q)))[first:]:
                k = q * GROUP + j
                remote(
                    out_buf.at[h, k], in_buf.at[h, k], out_sem.at[h], in_sem.at[h, q], place
                ).start()

        pack(0)
        pack(1)
        between()
        local(out_buf.at[h, 0], in_buf.at[h, 0], in_sem.at[h, 0])
        start(0, 1)

        @functools.partial(each, 2, GROUPS)
        def _(q):
            pack(q)
            start(q - 1)

        start(GROUPS - 1)

    def send_stats(first, second):
        for c in range(CHIPS):
            stat_out[c, :, :NODES] = first[c : c + 1, :]
            stat_out[c, :, NODES:] = second[c : c + 1, :]
        local(stat_out.at[me], stat_in.at[0], stat_sem)
        others(
            ahead,
            lambda k, place: remote(
                stat_out.at[chip(place)], stat_in.at[k], small_sem.at[0], stat_sem, place
            ).start(),
        )

    def collect_part(h):
        per_row = NODES // PART
        group_rows = GROUP // per_row

        @functools.partial(each, 0, GROUPS)
        def _(q):
            slots = pl.ds(q * GROUP, GROUP)
            done(in_buf.at[h, slots], in_sem.at[h, q])
            chosen = jnp.concatenate(
                [
                    jnp.where(rows == part_places[h, q * group_rows + j], 1.0, 0.0).astype(BF16)
                    for j in range(group_rows)
                ],
                axis=1,
            )
            parts = in_buf[h, slots].reshape(GROUP * PART, NODES)
            acc[...] += dot(chosen, parts).reshape(LEVELS, GRID_A, NODES)

    def exchange(step):
        copies = [
            to_partner(
                acc.at[l],
                partner_acc.at[step, l],
                acc_send_sem.at[step, l],
                acc_sem.at[step, l],
            )
            for l in range(LEVELS)
        ]
        for copy in copies:
            copy.start()
        done(stat_in, stat_sem)
        stat_sum[step] = jnp.sum(stat_in[...], axis=0)
        total = to_partner(
            stat_sum.at[step], stat_partner.at[step], tot_send_sem.at[step], tot_sem.at[step]
        )
        total.start()
        return copies, total

    def axis_passes(fields):
        firsts = [
            dot(field.astype(BF16), all_b[l % 2, l // 2]).astype(BF16)
            for l, field in enumerate(fields)
        ]
        return [dot(mat_a[l], first).astype(BF16) for l, first in enumerate(firsts)]

    def grid_step(step, copies, beta):
        for copy in copies:
            copy.wait()
        fields = []
        for l in range(LEVELS):
            sums = acc[l] + partner_acc[step, l]
            if step:
                sums = sums + beta * node_sums[l]
            node_sums[l] = sums
            fields.append(sums)
        for l, spread in enumerate(axis_passes(fields)):
            passed[l] = spread
        fields = []
        for l in range(LEVELS):
            mixed = coupling_ref[l, 0] * passed[0].astype(F32)
            for m in range(1, LEVELS):
                mixed = mixed + coupling_ref[l, m] * passed[m].astype(F32)
            fields.append(mixed)
        for l, values in enumerate(axis_passes(fields)):
            grid_values[l * GRID_A : (l + 1) * GRID_A, :] = values

    def curvature():
        product = jnp.zeros((8, NODES), F32)
        for l in range(LEVELS):
            terms = node_sums[l] * grid_values[l * GRID_A : (l + 1) * GRID_A, :].astype(F32)
            product = product + jnp.sum(terms.reshape(GRID_A // 8, 8, NODES), axis=0)
        return jnp.sum(product)

    def send_back(h, between):
        def pick(q):
            slots = pl.ds(q * GROUP, GROUP)
            where = spread_places[slots, pl.ds(h * PART, PART)].reshape(GROUP * PART, NODES)
            chosen = jnp.concatenate(
                [
                    jnp.where(where == cols + float(l * NODES), 1.0, 0.0).astype(BF16)
                    for l in range(LEVELS)
                ],
                axis=1,
            )
            ret_buf[h, slots] = (
                dot(chosen, grid_values[...]).astype(BF16).reshape(GROUP, PART, NODES)
            )

        def start(q, first=0):
            for j, place in list(enumerate(behind(q)))[first:]:
                remote(
                    ret_buf.at[h, q * GROUP + j],
                    got_buf.at[h, me],
                    ret_sem.at[h],
                    got_sem.at[h, q],
                    place,
                ).start()

        pick(0)
        between()
        local(ret_buf.at[h, 0], got_buf.at[h, me], got_sem.at[h, 0])
        start(0, 1)
        pick(1)

        @functools.partial(each, 2, GROUPS)
        def _(q):
            start(q - 1)
            pick(q)

        start(GROUPS - 1)

    def send_coefs(step):
        local(coef_out.at[step], coef_in.at[step, me], coef_sem.at[step])
        others(
            behind,
            lambda k, place: remote(
                coef_out.at[step],
                coef_in.at[step, me],
                small_sem.at[1 + step],
                coef_sem.at[step],
                place,
            ).start(),
        )

    def receive_coefs(step):
        done(coef_in.at[step], coef_sem.at[step])
        for c in range(CHIPS):
            coef_rows[step, c : c + 1, :] = coef_in[step, c]

    def receive_part(h):
        @functools.partial(each, 0, GROUPS)
        def _(q):
            done(got_buf.at[h, pl.ds(q * GROUP, GROUP)], got_sem.at[h, q])
            for place in ahead(q):
                c = chip(place)
                turn[column(c, h), :] = got_buf[h, c].astype(F32)

    def over_part(h, body, carry):
        def step(p, carry):
            i = h * PAIRS * 2 + 2 * p
            return body((i, i + 1), carry)

        return lax.fori_loop(0, PAIRS, step, carry)

    def rhs_quads(quads, total):
        values = [rhs_ref[:, window(i)] for i in quads]
        spread_out(quads, values)
        for v in values:
            total = total + folded(v * v)
        return total

    zero = jnp.zeros((CHIPS, NODES), F32)
    total = zero
    for h in range(PARTS):
        for load in loads[h]:
            load.wait()
        total = over_part(h, rhs_quads, total)
        if h:
            send_part(h)
        else:
            send_part(h, lambda: pl.semaphore_wait(barrier, CHIPS))
            local(place_out, places.at[0], place_sem)
            local(axis_a_ref, all_a.at[core, x, mine], a_sem)
            local(axis_b_ref, all_b.at[core, x], b_sem)

            def introduce(k, place):
                remote(place_out, places.at[k], small_sem.at[3], place_sem, place).start()
                remote(
                    axis_a_ref, all_a.at[core, x, mine], small_sem.at[4], a_sem, place
                ).start()

            others(ahead, introduce)
            for d in range(1, SIDE):
                remote(
                    axis_b_ref, all_b.at[core, x], small_sem.at[5], b_sem, (z, y, x_ahead[d])
                ).start()
    send_stats(total, total)

    for c in range(CHIPS):
        noise_rows[c : c + 1, :] = jnp.full((1, NODES), noise_ref[c])
    acc[...] = jnp.zeros_like(acc)
    done(places, place_sem)

    @functools.partial(each, 0, CHIPS)
    def _(k):
        spread_places[k] = jnp.transpose(jnp.broadcast_to(places[k], (TILES, NODES)))

    first_half = lax.broadcasted_iota(jnp.int32, (1, NODES), 1) < PART

    @functools.partial(each, 0, CHIPS // 2)
    def _(r):
        even, odd = places[2 * r], places[2 * r + 1]
        part_places[0, r] = jnp.where(first_half, even, pltpu.roll(odd, PART, 1))
        part_places[1, r] = jnp.where(first_half, pltpu.roll(even, PART, 1), odd)

    done(all_a.at[core], a_sem)
    done(all_b.at[core], b_sem)
    shared = [
        to_partner(all_a.at[core], all_a.at[core], small_sem.at[6], ab_sem.at[0]),
        to_partner(all_b.at[core], all_b.at[core], small_sem.at[7], ab_sem.at[1]),
    ]
    for copy in shared:
        copy.start()
    collect_part(0)
    for copy in shared:
        copy.wait()
    for l in range(LEVELS):
        mat_a[l] = all_a[l % 2, l // 2].astype(F32).reshape(GRID_A, GRID_A).astype(BF16)
    for h in range(1, PARTS):
        collect_part(h)
    copies, total = exchange(0)
    grid_step(0, copies, None)
    total.wait()
    norm_first = jnp.sum((stat_sum[0] + stat_partner[0])[:, :NODES])
    my_noise = noise_ref[me]

    def first_coefs():
        alpha = jnp.full((1, NODES), norm_first) / jnp.full(
            (1, NODES), curvature() + my_noise * norm_first
        )
        coef_out[0] = two(alpha)

    send_back(0, first_coefs)
    send_coefs(0)
    for h in range(1, PARTS):
        send_back(h, lambda: None)

    def residual_quads(quads, carry):
        total, cross = carry
        backs = gather_back(quads)
        values = []
        for i, back in zip(quads, backs):
            start = rhs_ref[:, window(i)]
            image = back + two(noise_rows[...]) * start
            v = start - coef_rows[0] * image
            residual_ref[:, window(i)] = v
            total = total + folded(v * v)
            cross = cross + folded(v * start)
            values.append(v)
        spread_out(quads, values)
        return total, cross

    acc[...] = jnp.zeros_like(acc)
    carry = (zero, zero)
    for h in range(PARTS):
        receive_part(h)
        if h == 0:
            receive_coefs(0)
        carry = over_part(h, residual_quads, carry)
        done(out_buf.at[h, rest], out_sem.at[h])
        send_part(h)
    done(stat_out.at[rest], small_sem.at[0])
    send_stats(*carry)
    for h in range(PARTS):
        collect_part(h)
    copies, total = exchange(1)
    total.wait()
    stats = stat_sum[1] + stat_partner[1]
    norm_next = jnp.sum(stats[:, :NODES])
    crossed = jnp.sum(stats[:, NODES:])
    beta = jnp.full((1, NODES), norm_next) / jnp.full((1, NODES), norm_first)
    grid_step(1, copies, beta)

    def second_coefs():
        length = norm_next + 2.0 * beta * crossed + beta * beta * norm_first
        alpha = jnp.full((1, NODES), norm_next) / (curvature() + my_noise * length)
        coef_out[1] = jnp.concatenate([alpha, beta], axis=1)

    for h in range(PARTS):
        done(ret_buf.at[h, rest], ret_sem.at[h])
    send_back(0, second_coefs)
    send_coefs(1)
    for h in range(1, PARTS):
        send_back(h, lambda: None)

    def ready_quads(quads, carry):
        alpha, beta = two(coef_rows[1, :, :NODES]), two(coef_rows[1, :, NODES:])
        for i in quads:
            start = rhs_ref[:, window(i)]
            left = residual_ref[:, window(i)]
            direction = left + beta * start
            step = alpha * direction
            solution_ref[:, window(i)] = coef_rows[0] * start + step
            residual_ref[:, window(i)] = left - two(noise_rows[...]) * step
        return carry

    def final_quads(quads, carry):
        alpha = two(coef_rows[1, :, :NODES])
        for i, back in zip(quads, gather_back(quads)):
            residual_ref[:, window(i)] = residual_ref[:, window(i)] - alpha * back
        return carry

    for h in range(PARTS):
        receive_part(h)
        if h == 0:
            receive_coefs(1)
            for p in range(PARTS):
                over_part(p, ready_quads, 0)
        over_part(h, final_quads, 0)

    for h in range(PARTS):
        done(out_buf.at[h, rest], out_sem.at[h])
        done(ret_buf.at[h, rest], ret_sem.at[h])
    done(stat_out.at[rest], small_sem.at[0])
    for step in range(2):
        done(coef_in.at[step, rest], small_sem.at[1 + step])
    done(places.at[rest], small_sem.at[3])
    done(turn.at[pl.ds(0, (CHIPS - 1) * 4)], small_sem.at[4])
    done(all_b.at[0, pl.ds(1, SIDE - 1)], small_sem.at[5])


def on_device(rhs, tile_weights, tile_owner, tile_row, axis_a, axis_b, coupling, noise):
    tile_count, tile_obs, node_cols = tile_weights.shape
    columns, width = rhs.shape
    a_rows, lvl_here, grid_first = axis_a.shape
    anywhere = pl.BlockSpec(memory_space=pltpu.HBM)
    vmem = pl.BlockSpec(memory_space=pltpu.VMEM)
    smem = pl.BlockSpec(memory_space=pltpu.SMEM)
    dma = pltpu.SemaphoreType.DMA
    whole = pltpu.VMEM((columns, width), F32)
    parts = pltpu.VMEM((PARTS, CHIPS, PART, NODES), BF16)
    field = pltpu.VMEM((LEVELS, GRID_A, NODES), F32)
    return pl.pallas_call(
        kernel,
        out_shape=(whole, whole),
        in_specs=[anywhere, anywhere, vmem, vmem, vmem, vmem, smem, smem],
        out_specs=(vmem, vmem),
        scratch_shapes=[
            whole,
            pltpu.VMEM((tile_count * tile_obs, node_cols), BF16),
            pltpu.VMEM((CHIPS * PITCH, NODES), F32),
            parts,
            parts,
            parts,
            parts,
            pltpu.VMEM((1, TILES), F32),
            pltpu.VMEM((CHIPS, 1, TILES), F32),
            pltpu.VMEM((PARTS, CHIPS // 2, 1, NODES), F32),
            pltpu.VMEM((CHIPS, TILES, NODES), F32),
            pltpu.VMEM((2, SIDE, SIDE * SIDE, a_rows, grid_first), BF16),
            pltpu.VMEM((2, SIDE, NODES, NODES), BF16),
            pltpu.VMEM((LEVELS, GRID_A, GRID_A), BF16),
            field,
            field,
            pltpu.VMEM((2, LEVELS, GRID_A, NODES), F32),
            pltpu.VMEM((LEVELS * GRID_A, NODES), BF16),
            pltpu.VMEM((LEVELS, GRID_A, NODES), BF16),
            pltpu.VMEM((CHIPS, NODES), F32),
            pltpu.VMEM((CHIPS, 1, 2 * NODES), F32),
            pltpu.VMEM((CHIPS, 1, 2 * NODES), F32),
            pltpu.VMEM((2, 1, 2 * NODES), F32),
            pltpu.VMEM((2, 1, 2 * NODES), F32),
            pltpu.VMEM((2, 1, 2 * NODES), F32),
            pltpu.VMEM((2, CHIPS, 1, 2 * NODES), F32),
            pltpu.VMEM((2, CHIPS, 2 * NODES), F32),
            dma((2, PARTS)),
            dma((PARTS,)),
            dma((PARTS, GROUPS)),
            dma((PARTS,)),
            dma((PARTS, GROUPS)),
            dma,
            dma,
            dma,
            dma((2,)),
            dma((8,)),
            dma,
            dma((2,)),
            dma((2, LEVELS)),
            dma((2, LEVELS)),
            dma((2,)),
            dma((2,)),
        ],
        compiler_params=pltpu.CompilerParams(
            collective_id=0, has_side_effects=True, vmem_limit_bytes=59 << 20
        ),
        name="conjugate_gradients",
    )(
        rhs,
        tile_weights.reshape(tile_count * tile_obs, node_cols),
        tile_owner.reshape(1, tile_count),
        tile_row.reshape(1, tile_count),
        axis_a.reshape(a_rows, grid_first),
        axis_b.reshape(node_cols, node_cols),
        coupling,
        noise,
    )


def solution(mesh):
    split = Mesh(mesh.devices.reshape(SIDE, SIDE, SIDE, 2), AXES)
    in_specs = (
        P(None, AXES),
        P(AXES, None, None),
        P(AXES, None),
        P(AXES),
        P(OBS, LVL, None),
        P(LVL, None, None),
        P(),
        P(),
    )
    out_specs = (P(None, AXES), P(None, AXES))
    return jax.shard_map(
        on_device, mesh=split, in_specs=in_specs, out_specs=out_specs, check_vma=False
    )
```

```python
import functools

import jax
import jax.numpy as jnp
from jax import lax
from jax.experimental import pallas as pl
from jax.experimental.pallas import tpu as pltpu
from jax.sharding import Mesh
from jax.sharding import PartitionSpec as P

AXES = ("obs_0", "obs_1", "lvl_0", "lvl_1")
OBS = ("obs_0", "obs_1")
LVL = ("lvl_0", "lvl_1")
MESH = pl.DeviceIdType.MESH

SIDE = 4
CHIPS = SIDE**3
LEVELS = 8
GRID_A = 128
NODES = 128
TILES = 128
TILE_OBS = 64
PARTS = 2
PART = TILES // PARTS
GROUP = 8
GROUPS = CHIPS // GROUP
QUAD = 4
WIDTH = QUAD * TILE_OBS
PAIRS = PART // QUAD // 2
PITCH = TILES + 8
F32 = jnp.float32
BF16 = jnp.bfloat16


def dot(a, b):
    return jnp.dot(a, b, preferred_element_type=F32)


def two(v):
    return jnp.concatenate([v, v], axis=1)


def kernel(
    rhs_hbm,
    weights_hbm,
    owner_ref,
    row_ref,
    axis_a_ref,
    axis_b_ref,
    coupling_ref,
    noise_ref,
    solution_ref,
    residual_ref,
    rhs_ref,
    weights_ref,
    turn,
    out_buf,
    in_buf,
    ret_buf,
    got_buf,
    place_out,
    places,
    part_places,
    spread_places,
    all_a,
    all_b,
    mat_a,
    acc,
    node_sums,
    partner_acc,
    grid_values,
    passed,
    noise_rows,
    stat_out,
    stat_in,
    stat_sum,
    stat_partner,
    coef_out,
    coef_in,
    coef_rows,
    load_sem,
    out_sem,
    in_sem,
    ret_sem,
    got_sem,
    place_sem,
    a_sem,
    b_sem,
    ab_sem,
    small_sem,
    stat_sem,
    coef_sem,
    acc_send_sem,
    acc_sem,
    tot_send_sem,
    tot_sem,
):
    z, y, x, core = (lax.axis_index(a) for a in AXES)
    me = (z * SIDE + y) * SIDE + x
    mine = z * SIDE + y
    way = 1 - 2 * core
    x_ahead = [lax.rem(x + SIDE + way * d, SIDE) for d in range(SIDE)]
    x_behind = [lax.rem(x + SIDE - way * d, SIDE) for d in range(SIDE)]

    def ahead(q):
        places = []
        for j in range(GROUP):
            low, mid = (0, 1, 3, 2)[j % SIDE], 2 * lax.rem(q, 2) + j // SIDE
            high = lax.div(q, 2)
            places.append(
                (
                    lax.rem(z + 12 + way * (high + mid + low), SIDE),
                    lax.rem(y + 12 + way * (mid + 2 * low), SIDE),
                    x_ahead[low],
                )
            )
        return places

    def behind(q):
        places = []
        for j in range(GROUP):
            low, mid = (0, 1, 3, 2)[j % SIDE], 2 * lax.rem(q, 2) + j // SIDE
            high = lax.div(q, 2)
            places.append(
                (
                    lax.rem(z + 12 - way * (high + mid + low), SIDE),
                    lax.rem(y + 12 - way * (mid + 2 * low), SIDE),
                    x_behind[low],
                )
            )
        return places

    def chip(place):
        return (place[0] * SIDE + place[1]) * SIDE + place[2]

    def remote(src, dst, send, recv, place):
        return pltpu.make_async_remote_copy(
            src, dst, send, recv, device_id=(*place, core), device_id_type=MESH
        )

    def to_partner(src, dst, send, recv):
        return pltpu.make_async_remote_copy(
            src, dst, send, recv, device_id=(z, y, x, 1 - core), device_id_type=MESH
        )

    def local(src, dst, sem):
        pltpu.make_async_copy(src, dst, sem).start()

    def done(ref, sem):
        pltpu.make_async_copy(ref, ref, sem).wait()

    def each(start, stop, body):
        def step(k, unused):
            body(k)
            return unused

        lax.fori_loop(start, stop, step, 0)

    def others(places_of, body):
        def group(q, first):
            places = places_of(q)
            for j in range(first, GROUP):
                body(q * GROUP + j, places[j])

        group(0, 1)
        each(1, GROUPS, lambda q: group(q, 0))

    loads = []
    for h in range(PARTS):
        obs = pl.ds(h * PART * TILE_OBS, PART * TILE_OBS)
        loads.append(
            (
                pltpu.make_async_copy(rhs_hbm.at[:, obs], rhs_ref.at[:, obs], load_sem.at[0, h]),
                pltpu.make_async_copy(
                    weights_hbm.at[obs], weights_ref.at[obs], load_sem.at[1, h]
                ),
            )
        )
        for load in loads[h]:
            load.start()
    barrier = pltpu.get_barrier_semaphore()

    def greet(place):
        pl.semaphore_signal(barrier, inc=1, device_id=place, device_id_type=MESH)

    around = [[lax.rem(v + d, SIDE) for d in range(SIDE)] for v in (z, y, x)]
    for k in range(CHIPS - 1, 0, -1):
        dz, dy, dx = k // (SIDE * SIDE), k // SIDE % SIDE, k % SIDE
        greet((around[0][dz], around[1][dy], around[2][dx], core))
    greet((z, y, x, 1 - core))

    lane = lax.broadcasted_iota(jnp.int32, (CHIPS, WIDTH), 1)
    in_tile = [lane // TILE_OBS == q for q in range(QUAD)]
    half = lax.broadcasted_iota(jnp.int32, (CHIPS, NODES), 1) < TILE_OBS
    rows = lax.broadcasted_iota(jnp.int32, (LEVELS * GRID_A, NODES), 0).astype(F32)
    cols = lax.broadcasted_iota(jnp.int32, (GROUP * PART, NODES), 1).astype(F32)
    rest = pl.ds(1, CHIPS - 1)

    owner = owner_ref[...]
    base = (owner & (LEVELS - 1)) * GRID_A + (owner >> 3) * (GRID_A // 16)
    place_out[...] = (base + row_ref[...]).astype(F32)

    def window(i):
        return pl.ds(pl.multiple_of(i * WIDTH, WIDTH), WIDTH)

    def column(c, h):
        return pl.ds(pl.multiple_of(c * PITCH + h * PART, 8), PART)

    def tile(t):
        return pl.ds(t, CHIPS, stride=PITCH)

    def spread_out(quads, values):
        parts = []
        for i, v in zip(quads, values):
            low = jnp.concatenate(
                [jnp.where(m, v, 0.0).astype(BF16) for m in in_tile], axis=0
            )
            parts.append(dot(low, weights_ref[window(i), :]))
        for i, part in zip(quads, parts):
            for q in range(QUAD):
                turn[tile(QUAD * i + q), :] = part[q * CHIPS : (q + 1) * CHIPS]

    def gather_back(quads):
        fulls = []
        for i in quads:
            values = jnp.concatenate(
                [turn[tile(QUAD * i + q), :].astype(BF16) for q in range(QUAD)], axis=0
            )
            fulls.append(
                lax.dot_general(
                    values,
                    weights_ref[window(i), :],
                    (((1,), (1,)), ((), ())),
                    preferred_element_type=F32,
                )
            )
        out = []
        for full in fulls:
            parts = []
            for p in range(QUAD // 2):
                lanes = slice(p * NODES, (p + 1) * NODES)
                even = full[2 * p * CHIPS : (2 * p + 1) * CHIPS, lanes]
                odd = full[(2 * p + 1) * CHIPS : (2 * p + 2) * CHIPS, lanes]
                parts.append(jnp.where(half, even, odd))
            out.append(jnp.concatenate(parts, axis=1))
        return out

    def folded(product):
        return product[:, :NODES] + product[:, NODES:]

    def send_part(h):
        def pack(q):
            for j, place in enumerate(ahead(q)):
                out_buf[h, q * GROUP + j] = turn[column(chip(place), h), :].astype(BF16)

        def start(q, first=0):
            for j, place in list(enumerate(ahead(q)))[first:]:
                k = q * GROUP + j
                remote(
                    out_buf.at[h, k], in_buf.at[h, k], out_sem.at[h], in_sem.at[h, q], place
                ).start()

        pack(0)
        pack(1)
        local(out_buf.at[h, 0], in_buf.at[h, 0], in_sem.at[h, 0])
        start(0, 1)

        @functools.partial(each, 2, GROUPS)
        def _(q):
            pack(q)
            start(q - 1)

        start(GROUPS - 1)

    def send_stats(first, second):
        for c in range(CHIPS):
            stat_out[c, :, :NODES] = first[c : c + 1, :]
            stat_out[c, :, NODES:] = second[c : c + 1, :]
        local(stat_out.at[me], stat_in.at[0], stat_sem)
        others(
            ahead,
            lambda k, place: remote(
                stat_out.at[chip(place)], stat_in.at[k], small_sem.at[0], stat_sem, place
            ).start(),
        )

    def collect_part(h):
        per_row = NODES // PART
        group_rows = GROUP // per_row

        @functools.partial(each, 0, GROUPS)
        def _(q):
            slots = pl.ds(q * GROUP, GROUP)
            done(in_buf.at[h, slots], in_sem.at[h, q])
            chosen = jnp.concatenate(
                [
                    jnp.where(rows == part_places[h, q * group_rows + j], 1.0, 0.0).astype(BF16)
                    for j in range(group_rows)
                ],
                axis=1,
            )
            parts = in_buf[h, slots].reshape(GROUP * PART, NODES)
            acc[...] += dot(chosen, parts).reshape(LEVELS, GRID_A, NODES)

    def exchange(step):
        copies = [
            to_partner(
                acc.at[l],
                partner_acc.at[step, l],
                acc_send_sem.at[step, l],
                acc_sem.at[step, l],
            )
            for l in range(LEVELS)
        ]
        for copy in copies:
            copy.start()
        done(stat_in, stat_sem)
        stat_sum[step] = jnp.sum(stat_in[...], axis=0)
        total = to_partner(
            stat_sum.at[step], stat_partner.at[step], tot_send_sem.at[step], tot_sem.at[step]
        )
        total.start()
        return copies, total

    def axis_passes(fields):
        firsts = [
            dot(field.astype(BF16), all_b[l % 2, l // 2]).astype(BF16)
            for l, field in enumerate(fields)
        ]
        return [dot(mat_a[l], first).astype(BF16) for l, first in enumerate(firsts)]

    def grid_step(step, copies, beta):
        for copy in copies:
            copy.wait()
        fields = []
        for l in range(LEVELS):
            sums = acc[l] + partner_acc[step, l]
            if step:
                sums = sums + beta * node_sums[l]
            node_sums[l] = sums
            fields.append(sums)
        for l, spread in enumerate(axis_passes(fields)):
            passed[l] = spread
        fields = []
        for l in range(LEVELS):
            mixed = coupling_ref[l, 0] * passed[0].astype(F32)
            for m in range(1, LEVELS):
                mixed = mixed + coupling_ref[l, m] * passed[m].astype(F32)
            fields.append(mixed)
        for l, values in enumerate(axis_passes(fields)):
            grid_values[l * GRID_A : (l + 1) * GRID_A, :] = values

    def curvature():
        product = jnp.zeros((8, NODES), F32)
        for l in range(LEVELS):
            terms = node_sums[l] * grid_values[l * GRID_A : (l + 1) * GRID_A, :].astype(F32)
            product = product + jnp.sum(terms.reshape(GRID_A // 8, 8, NODES), axis=0)
        return jnp.sum(product)

    def send_back(h, between):
        def pick(q):
            slots = pl.ds(q * GROUP, GROUP)
            where = spread_places[slots, pl.ds(h * PART, PART)].reshape(GROUP * PART, NODES)
            chosen = jnp.concatenate(
                [
                    jnp.where(where == cols + float(l * NODES), 1.0, 0.0).astype(BF16)
                    for l in range(LEVELS)
                ],
                axis=1,
            )
            ret_buf[h, slots] = (
                dot(chosen, grid_values[...]).astype(BF16).reshape(GROUP, PART, NODES)
            )

        def start(q, first=0):
            for j, place in list(enumerate(behind(q)))[first:]:
                remote(
                    ret_buf.at[h, q * GROUP + j],
                    got_buf.at[h, me],
                    ret_sem.at[h],
                    got_sem.at[h, q],
                    place,
                ).start()

        pick(0)
        between()
        local(ret_buf.at[h, 0], got_buf.at[h, me], got_sem.at[h, 0])
        start(0, 1)
        pick(1)

        @functools.partial(each, 2, GROUPS)
        def _(q):
            start(q - 1)
            pick(q)

        start(GROUPS - 1)

    def send_coefs(step):
        local(coef_out.at[step], coef_in.at[step, me], coef_sem.at[step])
        others(
            behind,
            lambda k, place: remote(
                coef_out.at[step],
                coef_in.at[step, me],
                small_sem.at[1 + step],
                coef_sem.at[step],
                place,
            ).start(),
        )

    def receive_coefs(step):
        done(coef_in.at[step], coef_sem.at[step])
        for c in range(CHIPS):
            coef_rows[step, c : c + 1, :] = coef_in[step, c]

    def receive_part(h):
        @functools.partial(each, 0, GROUPS)
        def _(q):
            done(got_buf.at[h, pl.ds(q * GROUP, GROUP)], got_sem.at[h, q])
            for place in ahead(q):
                c = chip(place)
                turn[column(c, h), :] = got_buf[h, c].astype(F32)

    def over_part(h, body, carry):
        def step(p, carry):
            i = h * PAIRS * 2 + 2 * p
            return body((i, i + 1), carry)

        return lax.fori_loop(0, PAIRS, step, carry)

    def rhs_quads(quads, total):
        values = [rhs_ref[:, window(i)] for i in quads]
        spread_out(quads, values)
        for v in values:
            total = total + folded(v * v)
        return total

    zero = jnp.zeros((CHIPS, NODES), F32)
    total = zero
    for h in range(PARTS):
        for load in loads[h]:
            load.wait()
        total = over_part(h, rhs_quads, total)
        if h == 0:
            pl.semaphore_wait(barrier, CHIPS)
        send_part(h)
        if h == 0:
            local(place_out, places.at[0], place_sem)
            local(axis_a_ref, all_a.at[core, x, mine], a_sem)
            local(axis_b_ref, all_b.at[core, x], b_sem)

            def introduce(k, place):
                remote(place_out, places.at[k], small_sem.at[3], place_sem, place).start()
                remote(
                    axis_a_ref, all_a.at[core, x, mine], small_sem.at[4], a_sem, place
                ).start()

            others(ahead, introduce)
            for d in range(1, SIDE):
                remote(
                    axis_b_ref, all_b.at[core, x], small_sem.at[5], b_sem, (z, y, x_ahead[d])
                ).start()
    send_stats(total, total)

    for c in range(CHIPS):
        noise_rows[c : c + 1, :] = jnp.full((1, NODES), noise_ref[c])
    acc[...] = jnp.zeros_like(acc)
    done(places, place_sem)

    @functools.partial(each, 0, CHIPS)
    def _(k):
        spread_places[k] = jnp.transpose(jnp.broadcast_to(places[k], (TILES, NODES)))

    first_half = lax.broadcasted_iota(jnp.int32, (1, NODES), 1) < PART

    @functools.partial(each, 0, CHIPS // 2)
    def _(r):
        even, odd = places[2 * r], places[2 * r + 1]
        part_places[0, r] = jnp.where(first_half, even, pltpu.roll(odd, PART, 1))
        part_places[1, r] = jnp.where(first_half, pltpu.roll(even, PART, 1), odd)

    done(all_a.at[core], a_sem)
    done(all_b.at[core], b_sem)
    shared = [
        to_partner(all_a.at[core], all_a.at[core], small_sem.at[6], ab_sem.at[0]),
        to_partner(all_b.at[core], all_b.at[core], small_sem.at[7], ab_sem.at[1]),
    ]
    for copy in shared:
        copy.start()
    collect_part(0)
    for copy in shared:
        copy.wait()
    for l in range(LEVELS):
        mat_a[l] = all_a[l % 2, l // 2].astype(F32).reshape(GRID_A, GRID_A).astype(BF16)
    for h in range(1, PARTS):
        collect_part(h)
    copies, total = exchange(0)
    grid_step(0, copies, None)
    total.wait()
    norm_first = jnp.sum((stat_sum[0] + stat_partner[0])[:, :NODES])
    my_noise = noise_ref[me]

    def first_coefs():
        alpha = jnp.full((1, NODES), norm_first) / jnp.full(
            (1, NODES), curvature() + my_noise * norm_first
        )
        coef_out[0] = two(alpha)

    send_back(0, first_coefs)
    send_coefs(0)
    for h in range(1, PARTS):
        send_back(h, lambda: None)

    def residual_quads(quads, carry):
        total, cross = carry
        backs = gather_back(quads)
        values = []
        for i, back in zip(quads, backs):
            start = rhs_ref[:, window(i)]
            image = back + two(noise_rows[...]) * start
            v = start - coef_rows[0] * image
            residual_ref[:, window(i)] = v
            total = total + folded(v * v)
            cross = cross + folded(v * start)
            values.append(v)
        spread_out(quads, values)
        return total, cross

    acc[...] = jnp.zeros_like(acc)
    carry = (zero, zero)
    for h in range(PARTS):
        receive_part(h)
        if h == 0:
            receive_coefs(0)
        carry = over_part(h, residual_quads, carry)
        done(out_buf.at[h, rest], out_sem.at[h])
        send_part(h)
    done(stat_out.at[rest], small_sem.at[0])
    send_stats(*carry)
    for h in range(PARTS):
        collect_part(h)
    copies, total = exchange(1)
    total.wait()
    stats = stat_sum[1] + stat_partner[1]
    norm_next = jnp.sum(stats[:, :NODES])
    crossed = jnp.sum(stats[:, NODES:])
    beta = jnp.full((1, NODES), norm_next) / jnp.full((1, NODES), norm_first)
    grid_step(1, copies, beta)

    def second_coefs():
        length = norm_next + 2.0 * beta * crossed + beta * beta * norm_first
        alpha = jnp.full((1, NODES), norm_next) / (curvature() + my_noise * length)
        coef_out[1] = jnp.concatenate([alpha, beta], axis=1)

    for h in range(PARTS):
        done(ret_buf.at[h, rest], ret_sem.at[h])
    send_back(0, second_coefs)
    send_coefs(1)
    for h in range(1, PARTS):
        send_back(h, lambda: None)

    def ready_quads(quads, carry):
        alpha, beta = two(coef_rows[1, :, :NODES]), two(coef_rows[1, :, NODES:])
        for i in quads:
            start = rhs_ref[:, window(i)]
            left = residual_ref[:, window(i)]
            direction = left + beta * start
            step = alpha * direction
            solution_ref[:, window(i)] = coef_rows[0] * start + step
            residual_ref[:, window(i)] = left - two(noise_rows[...]) * step
        return carry

    def final_quads(quads, carry):
        alpha = two(coef_rows[1, :, :NODES])
        for i, back in zip(quads, gather_back(quads)):
            residual_ref[:, window(i)] = residual_ref[:, window(i)] - alpha * back
        return carry

    for h in range(PARTS):
        receive_part(h)
        if h == 0:
            receive_coefs(1)
            for p in range(PARTS):
                over_part(p, ready_quads, 0)
        over_part(h, final_quads, 0)

    for h in range(PARTS):
        done(out_buf.at[h, rest], out_sem.at[h])
        done(ret_buf.at[h, rest], ret_sem.at[h])
    done(stat_out.at[rest], small_sem.at[0])
    for step in range(2):
        done(coef_in.at[step, rest], small_sem.at[1 + step])
    done(places.at[rest], small_sem.at[3])
    done(turn.at[pl.ds(0, (CHIPS - 1) * 4)], small_sem.at[4])
    done(all_b.at[0, pl.ds(1, SIDE - 1)], small_sem.at[5])


def on_device(rhs, tile_weights, tile_owner, tile_row, axis_a, axis_b, coupling, noise):
    tile_count, tile_obs, node_cols = tile_weights.shape
    columns, width = rhs.shape
    a_rows, lvl_here, grid_first = axis_a.shape
    anywhere = pl.BlockSpec(memory_space=pltpu.HBM)
    vmem = pl.BlockSpec(memory_space=pltpu.VMEM)
    smem = pl.BlockSpec(memory_space=pltpu.SMEM)
    dma = pltpu.SemaphoreType.DMA
    whole = pltpu.VMEM((columns, width), F32)
    parts = pltpu.VMEM((PARTS, CHIPS, PART, NODES), BF16)
    field = pltpu.VMEM((LEVELS, GRID_A, NODES), F32)
    return pl.pallas_call(
        kernel,
        out_shape=(whole, whole),
        in_specs=[anywhere, anywhere, vmem, vmem, vmem, vmem, smem, smem],
        out_specs=(vmem, vmem),
        scratch_shapes=[
            whole,
            pltpu.VMEM((tile_count * tile_obs, node_cols), BF16),
            pltpu.VMEM((CHIPS * PITCH, NODES), F32),
            parts,
            parts,
            parts,
            parts,
            pltpu.VMEM((1, TILES), F32),
            pltpu.VMEM((CHIPS, 1, TILES), F32),
            pltpu.VMEM((PARTS, CHIPS // 2, 1, NODES), F32),
            pltpu.VMEM((CHIPS, TILES, NODES), F32),
            pltpu.VMEM((2, SIDE, SIDE * SIDE, a_rows, grid_first), BF16),
            pltpu.VMEM((2, SIDE, NODES, NODES), BF16),
            pltpu.VMEM((LEVELS, GRID_A, GRID_A), BF16),
            field,
            field,
            pltpu.VMEM((2, LEVELS, GRID_A, NODES), F32),
            pltpu.VMEM((LEVELS * GRID_A, NODES), BF16),
            pltpu.VMEM((LEVELS, GRID_A, NODES), BF16),
            pltpu.VMEM((CHIPS, NODES), F32),
            pltpu.VMEM((CHIPS, 1, 2 * NODES), F32),
            pltpu.VMEM((CHIPS, 1, 2 * NODES), F32),
            pltpu.VMEM((2, 1, 2 * NODES), F32),
            pltpu.VMEM((2, 1, 2 * NODES), F32),
            pltpu.VMEM((2, 1, 2 * NODES), F32),
            pltpu.VMEM((2, CHIPS, 1, 2 * NODES), F32),
            pltpu.VMEM((2, CHIPS, 2 * NODES), F32),
            dma((2, PARTS)),
            dma((PARTS,)),
            dma((PARTS, GROUPS)),
            dma((PARTS,)),
            dma((PARTS, GROUPS)),
            dma,
            dma,
            dma,
            dma((2,)),
            dma((8,)),
            dma,
            dma((2,)),
            dma((2, LEVELS)),
            dma((2, LEVELS)),
            dma((2,)),
            dma((2,)),
        ],
        compiler_params=pltpu.CompilerParams(
            collective_id=0, has_side_effects=True, vmem_limit_bytes=59 << 20
        ),
        name="conjugate_gradients",
    )(
        rhs,
        tile_weights.reshape(tile_count * tile_obs, node_cols),
        tile_owner.reshape(1, tile_count),
        tile_row.reshape(1, tile_count),
        axis_a.reshape(a_rows, grid_first),
        axis_b.reshape(node_cols, node_cols),
        coupling,
        noise,
    )


def solution(mesh):
    split = Mesh(mesh.devices.reshape(SIDE, SIDE, SIDE, 2), AXES)
    in_specs = (
        P(None, AXES),
        P(AXES, None, None),
        P(AXES, None),
        P(AXES),
        P(OBS, LVL, None),
        P(LVL, None, None),
        P(),
        P(),
    )
    out_specs = (P(None, AXES), P(None, AXES))
    return jax.shard_map(
        on_device, mesh=split, in_specs=in_specs, out_specs=out_specs, check_vma=False
    )
```

```python
import functools

import jax
import jax.numpy as jnp
from jax import lax
from jax.experimental import pallas as pl
from jax.experimental.pallas import tpu as pltpu
from jax.sharding import Mesh
from jax.sharding import PartitionSpec as P

AXES = ("obs_0", "obs_1", "lvl_0", "lvl_1")
OBS = ("obs_0", "obs_1")
LVL = ("lvl_0", "lvl_1")
MESH = pl.DeviceIdType.MESH

SIDE = 4
CHIPS = SIDE**3
LEVELS = 8
GRID_A = 128
NODES = 128
TILES = 128
TILE_OBS = 64
PARTS = 2
PART = TILES // PARTS
GROUP = 8
GROUPS = CHIPS // GROUP
QUAD = 4
WIDTH = QUAD * TILE_OBS
PAIRS = PART // QUAD // 2
PITCH = TILES + 8
F32 = jnp.float32
BF16 = jnp.bfloat16


def dot(a, b):
    return jnp.dot(a, b, preferred_element_type=F32)


def two(v):
    return jnp.concatenate([v, v], axis=1)


def kernel(
    rhs_hbm,
    weights_hbm,
    owner_ref,
    row_ref,
    axis_a_ref,
    axis_b_ref,
    coupling_ref,
    noise_ref,
    solution_ref,
    residual_ref,
    rhs_ref,
    weights_ref,
    turn,
    out_buf,
    in_buf,
    ret_buf,
    got_buf,
    place_out,
    places,
    part_places,
    spread_places,
    all_a,
    all_b,
    mat_a,
    acc,
    low_acc,
    node_sums,
    partner_acc,
    grid_values,
    passed,
    noise_rows,
    stat_out,
    stat_in,
    stat_sum,
    stat_partner,
    coef_out,
    coef_in,
    coef_rows,
    load_sem,
    out_sem,
    in_sem,
    ret_sem,
    got_sem,
    place_sem,
    a_sem,
    b_sem,
    ab_sem,
    small_sem,
    stat_sem,
    coef_sem,
    acc_send_sem,
    acc_sem,
    tot_send_sem,
    tot_sem,
):
    z, y, x, core = (lax.axis_index(a) for a in AXES)
    me = (z * SIDE + y) * SIDE + x
    mine = z * SIDE + y
    way = 1 - 2 * core
    x_ahead = [lax.rem(x + SIDE + way * d, SIDE) for d in range(SIDE)]
    x_behind = [lax.rem(x + SIDE - way * d, SIDE) for d in range(SIDE)]

    def ahead(q):
        places = []
        for j in range(GROUP):
            low, mid = (0, 1, 3, 2)[j % SIDE], 2 * lax.rem(q, 2) + j // SIDE
            high = lax.div(q, 2)
            places.append(
                (
                    lax.rem(z + 12 + way * (high + mid + low), SIDE),
                    lax.rem(y + 12 + way * (mid + 2 * low), SIDE),
                    x_ahead[low],
                )
            )
        return places

    def behind(q):
        places = []
        for j in range(GROUP):
            low, mid = (0, 1, 3, 2)[j % SIDE], 2 * lax.rem(q, 2) + j // SIDE
            high = lax.div(q, 2)
            places.append(
                (
                    lax.rem(z + 12 - way * (high + mid + low), SIDE),
                    lax.rem(y + 12 - way * (mid + 2 * low), SIDE),
                    x_behind[low],
                )
            )
        return places

    def chip(place):
        return (place[0] * SIDE + place[1]) * SIDE + place[2]

    def remote(src, dst, send, recv, place):
        return pltpu.make_async_remote_copy(
            src, dst, send, recv, device_id=(*place, core), device_id_type=MESH
        )

    def to_partner(src, dst, send, recv):
        return pltpu.make_async_remote_copy(
            src, dst, send, recv, device_id=(z, y, x, 1 - core), device_id_type=MESH
        )

    def local(src, dst, sem):
        pltpu.make_async_copy(src, dst, sem).start()

    def done(ref, sem):
        pltpu.make_async_copy(ref, ref, sem).wait()

    def each(start, stop, body):
        def step(k, unused):
            body(k)
            return unused

        lax.fori_loop(start, stop, step, 0)

    def others(places_of, body):
        def group(q, first):
            places = places_of(q)
            for j in range(first, GROUP):
                body(q * GROUP + j, places[j])

        group(0, 1)
        each(1, GROUPS, lambda q: group(q, 0))

    loads = []
    for h in range(PARTS):
        obs = pl.ds(h * PART * TILE_OBS, PART * TILE_OBS)
        loads.append(
            (
                pltpu.make_async_copy(rhs_hbm.at[:, obs], rhs_ref.at[:, obs], load_sem.at[0, h]),
                pltpu.make_async_copy(
                    weights_hbm.at[obs], weights_ref.at[obs], load_sem.at[1, h]
                ),
            )
        )
        for load in loads[h]:
            load.start()
    barrier = pltpu.get_barrier_semaphore()

    def greet(place):
        pl.semaphore_signal(barrier, inc=1, device_id=place, device_id_type=MESH)

    around = [[lax.rem(v + d, SIDE) for d in range(SIDE)] for v in (z, y, x)]
    for k in range(CHIPS - 1, 0, -1):
        dz, dy, dx = k // (SIDE * SIDE), k // SIDE % SIDE, k % SIDE
        greet((around[0][dz], around[1][dy], around[2][dx], core))
    greet((z, y, x, 1 - core))

    lane = lax.broadcasted_iota(jnp.int32, (CHIPS, WIDTH), 1)
    in_tile = [lane // TILE_OBS == q for q in range(QUAD)]
    half = lax.broadcasted_iota(jnp.int32, (CHIPS, NODES), 1) < TILE_OBS
    rows = lax.broadcasted_iota(jnp.int32, (LEVELS * GRID_A, NODES), 0).astype(F32)
    cols = lax.broadcasted_iota(jnp.int32, (GROUP * PART, NODES), 1).astype(F32)
    rest = pl.ds(1, CHIPS - 1)

    owner = owner_ref[...]
    base = (owner & (LEVELS - 1)) * GRID_A + (owner >> 3) * (GRID_A // 16)
    place_out[...] = (base + row_ref[...]).astype(F32)

    def window(i):
        return pl.ds(pl.multiple_of(i * WIDTH, WIDTH), WIDTH)

    def column(c, h):
        return pl.ds(pl.multiple_of(c * PITCH + h * PART, 8), PART)

    def tile(t):
        return pl.ds(t, CHIPS, stride=PITCH)

    def spread_out(quads, values):
        parts = []
        for i, v in zip(quads, values):
            low = jnp.concatenate(
                [jnp.where(m, v, 0.0).astype(BF16) for m in in_tile], axis=0
            )
            parts.append(dot(low, weights_ref[window(i), :]))
        for i, part in zip(quads, parts):
            for q in range(QUAD):
                turn[tile(QUAD * i + q), :] = part[q * CHIPS : (q + 1) * CHIPS]

    def gather_back(quads):
        fulls = []
        for i in quads:
            values = jnp.concatenate(
                [turn[tile(QUAD * i + q), :].astype(BF16) for q in range(QUAD)], axis=0
            )
            fulls.append(
                lax.dot_general(
                    values,
                    weights_ref[window(i), :],
                    (((1,), (1,)), ((), ())),
                    preferred_element_type=F32,
                )
            )
        out = []
        for full in fulls:
            parts = []
            for p in range(QUAD // 2):
                lanes = slice(p * NODES, (p + 1) * NODES)
                even = full[2 * p * CHIPS : (2 * p + 1) * CHIPS, lanes]
                odd = full[(2 * p + 1) * CHIPS : (2 * p + 2) * CHIPS, lanes]
                parts.append(jnp.where(half, even, odd))
            out.append(jnp.concatenate(parts, axis=1))
        return out

    def folded(product):
        return product[:, :NODES] + product[:, NODES:]

    def send_part(h):
        def pack(q):
            for j, place in enumerate(ahead(q)):
                out_buf[h, q * GROUP + j] = turn[column(chip(place), h), :].astype(BF16)

        def start(q, first=0):
            for j, place in list(enumerate(ahead(q)))[first:]:
                k = q * GROUP + j
                remote(
                    out_buf.at[h, k], in_buf.at[h, k], out_sem.at[h], in_sem.at[h, q], place
                ).start()

        pack(0)
        pack(1)
        local(out_buf.at[h, 0], in_buf.at[h, 0], in_sem.at[h, 0])
        start(0, 1)

        @functools.partial(each, 2, GROUPS)
        def _(q):
            pack(q)
            start(q - 1)

        start(GROUPS - 1)

    def send_stats(first, second):
        for c in range(CHIPS):
            stat_out[c, :, :NODES] = first[c : c + 1, :]
            stat_out[c, :, NODES:] = second[c : c + 1, :]
        local(stat_out.at[me], stat_in.at[0], stat_sem)
        others(
            ahead,
            lambda k, place: remote(
                stat_out.at[chip(place)], stat_in.at[k], small_sem.at[0], stat_sem, place
            ).start(),
        )

    def collect_part(h):
        per_row = NODES // PART
        group_rows = GROUP // per_row

        @functools.partial(each, 0, GROUPS)
        def _(q):
            slots = pl.ds(q * GROUP, GROUP)
            done(in_buf.at[h, slots], in_sem.at[h, q])
            chosen = jnp.concatenate(
                [
                    jnp.where(rows == part_places[h, q * group_rows + j], 1.0, 0.0).astype(BF16)
                    for j in range(group_rows)
                ],
                axis=1,
            )
            parts = in_buf[h, slots].reshape(GROUP * PART, NODES)
            acc[...] += dot(chosen, parts).reshape(LEVELS, GRID_A, NODES)

    def exchange(step):
        low_acc[...] = acc[...].astype(BF16)
        copies = [
            to_partner(
                low_acc.at[l],
                partner_acc.at[step, l],
                acc_send_sem.at[step, l],
                acc_sem.at[step, l],
            )
            for l in range(LEVELS)
        ]
        for copy in copies:
            copy.start()
        done(stat_in, stat_sem)
        stat_sum[step] = jnp.sum(stat_in[...], axis=0)
        total = to_partner(
            stat_sum.at[step], stat_partner.at[step], tot_send_sem.at[step], tot_sem.at[step]
        )
        total.start()
        return copies, total

    def axis_passes(fields):
        firsts = [
            dot(field.astype(BF16), all_b[l % 2, l // 2]).astype(BF16)
            for l, field in enumerate(fields)
        ]
        return [dot(mat_a[l], first).astype(BF16) for l, first in enumerate(firsts)]

    def grid_step(step, copies, beta):
        for copy in copies:
            copy.wait()
        fields = []
        for l in range(LEVELS):
            sums = low_acc[l].astype(F32) + partner_acc[step, l].astype(F32)
            if step:
                sums = sums + beta * node_sums[l]
            node_sums[l] = sums
            fields.append(sums)
        for l, spread in enumerate(axis_passes(fields)):
            passed[l] = spread
        fields = []
        for l in range(LEVELS):
            mixed = coupling_ref[l, 0] * passed[0].astype(F32)
            for m in range(1, LEVELS):
                mixed = mixed + coupling_ref[l, m] * passed[m].astype(F32)
            fields.append(mixed)
        for l, values in enumerate(axis_passes(fields)):
            grid_values[l * GRID_A : (l + 1) * GRID_A, :] = values

    def curvature():
        product = jnp.zeros((8, NODES), F32)
        for l in range(LEVELS):
            terms = node_sums[l] * grid_values[l * GRID_A : (l + 1) * GRID_A, :].astype(F32)
            product = product + jnp.sum(terms.reshape(GRID_A // 8, 8, NODES), axis=0)
        return jnp.sum(product)

    def send_back(h, between):
        def pick(q):
            slots = pl.ds(q * GROUP, GROUP)
            where = spread_places[slots, pl.ds(h * PART, PART)].reshape(GROUP * PART, NODES)
            chosen = jnp.concatenate(
                [
                    jnp.where(where == cols + float(l * NODES), 1.0, 0.0).astype(BF16)
                    for l in range(LEVELS)
                ],
                axis=1,
            )
            ret_buf[h, slots] = (
                dot(chosen, grid_values[...]).astype(BF16).reshape(GROUP, PART, NODES)
            )

        def start(q, first=0):
            for j, place in list(enumerate(behind(q)))[first:]:
                remote(
                    ret_buf.at[h, q * GROUP + j],
                    got_buf.at[h, me],
                    ret_sem.at[h],
                    got_sem.at[h, q],
                    place,
                ).start()

        pick(0)
        local(ret_buf.at[h, 0], got_buf.at[h, me], got_sem.at[h, 0])
        start(0, 1)
        between()
        pick(1)

        @functools.partial(each, 2, GROUPS)
        def _(q):
            start(q - 1)
            pick(q)

        start(GROUPS - 1)

    def send_coefs(step):
        local(coef_out.at[step], coef_in.at[step, me], coef_sem.at[step])
        others(
            behind,
            lambda k, place: remote(
                coef_out.at[step],
                coef_in.at[step, me],
                small_sem.at[1 + step],
                coef_sem.at[step],
                place,
            ).start(),
        )

    def receive_coefs(step):
        done(coef_in.at[step], coef_sem.at[step])
        for c in range(CHIPS):
            coef_rows[step, c : c + 1, :] = coef_in[step, c]

    def receive_part(h):
        @functools.partial(each, 0, GROUPS)
        def _(q):
            done(got_buf.at[h, pl.ds(q * GROUP, GROUP)], got_sem.at[h, q])
            for place in ahead(q):
                c = chip(place)
                turn[column(c, h), :] = got_buf[h, c].astype(F32)

    def over_part(h, body, carry):
        def step(p, carry):
            i = h * PAIRS * 2 + 2 * p
            return body((i, i + 1), carry)

        return lax.fori_loop(0, PAIRS, step, carry)

    def rhs_quads(quads, total):
        values = [rhs_ref[:, window(i)] for i in quads]
        spread_out(quads, values)
        for v in values:
            total = total + folded(v * v)
        return total

    zero = jnp.zeros((CHIPS, NODES), F32)
    total = zero
    for h in range(PARTS):
        for load in loads[h]:
            load.wait()
        total = over_part(h, rhs_quads, total)
        if h == 0:
            pl.semaphore_wait(barrier, CHIPS)
        send_part(h)
        if h == 0:
            local(place_out, places.at[0], place_sem)
            local(axis_a_ref, all_a.at[core, x, mine], a_sem)
            local(axis_b_ref, all_b.at[core, x], b_sem)

            def introduce(k, place):
                remote(place_out, places.at[k], small_sem.at[3], place_sem, place).start()
                remote(
                    axis_a_ref, all_a.at[core, x, mine], small_sem.at[4], a_sem, place
                ).start()

            others(ahead, introduce)
            for d in range(1, SIDE):
                remote(
                    axis_b_ref, all_b.at[core, x], small_sem.at[5], b_sem, (z, y, x_ahead[d])
                ).start()
    send_stats(total, total)

    for c in range(CHIPS):
        noise_rows[c : c + 1, :] = jnp.full((1, NODES), noise_ref[c])
    acc[...] = jnp.zeros_like(acc)
    done(places, place_sem)

    @functools.partial(each, 0, CHIPS)
    def _(k):
        spread_places[k] = jnp.transpose(jnp.broadcast_to(places[k], (TILES, NODES)))

    first_half = lax.broadcasted_iota(jnp.int32, (1, NODES), 1) < PART

    @functools.partial(each, 0, CHIPS // 2)
    def _(r):
        even, odd = places[2 * r], places[2 * r + 1]
        part_places[0, r] = jnp.where(first_half, even, pltpu.roll(odd, PART, 1))
        part_places[1, r] = jnp.where(first_half, pltpu.roll(even, PART, 1), odd)

    done(all_a.at[core], a_sem)
    done(all_b.at[core], b_sem)
    shared = [
        to_partner(all_a.at[core], all_a.at[core], small_sem.at[6], ab_sem.at[0]),
        to_partner(all_b.at[core], all_b.at[core], small_sem.at[7], ab_sem.at[1]),
    ]
    for copy in shared:
        copy.start()
    collect_part(0)
    for copy in shared:
        copy.wait()
    for l in range(LEVELS):
        mat_a[l] = all_a[l % 2, l // 2].astype(F32).reshape(GRID_A, GRID_A).astype(BF16)
    for h in range(1, PARTS):
        collect_part(h)
    copies, total = exchange(0)
    grid_step(0, copies, None)
    total.wait()
    norm_first = jnp.sum((stat_sum[0] + stat_partner[0])[:, :NODES])
    my_noise = noise_ref[me]

    def first_coefs():
        alpha = jnp.full((1, NODES), norm_first) / jnp.full(
            (1, NODES), curvature() + my_noise * norm_first
        )
        coef_out[0] = two(alpha)

    send_back(0, first_coefs)
    send_coefs(0)
    for h in range(1, PARTS):
        send_back(h, lambda: None)

    def residual_quads(quads, carry):
        total, cross = carry
        backs = gather_back(quads)
        values = []
        for i, back in zip(quads, backs):
            start = rhs_ref[:, window(i)]
            image = back + two(noise_rows[...]) * start
            v = start - coef_rows[0] * image
            residual_ref[:, window(i)] = v
            total = total + folded(v * v)
            cross = cross + folded(v * start)
            values.append(v)
        spread_out(quads, values)
        return total, cross

    acc[...] = jnp.zeros_like(acc)
    carry = (zero, zero)
    for h in range(PARTS):
        receive_part(h)
        if h == 0:
            receive_coefs(0)
        carry = over_part(h, residual_quads, carry)
        done(out_buf.at[h, rest], out_sem.at[h])
        send_part(h)
    done(stat_out.at[rest], small_sem.at[0])
    send_stats(*carry)
    for h in range(PARTS):
        collect_part(h)
    copies, total = exchange(1)
    total.wait()
    stats = stat_sum[1] + stat_partner[1]
    norm_next = jnp.sum(stats[:, :NODES])
    crossed = jnp.sum(stats[:, NODES:])
    beta = jnp.full((1, NODES), norm_next) / jnp.full((1, NODES), norm_first)
    grid_step(1, copies, beta)

    def second_coefs():
        length = norm_next + 2.0 * beta * crossed + beta * beta * norm_first
        alpha = jnp.full((1, NODES), norm_next) / (curvature() + my_noise * length)
        coef_out[1] = jnp.concatenate([alpha, beta], axis=1)

    for h in range(PARTS):
        done(ret_buf.at[h, rest], ret_sem.at[h])
    send_back(0, second_coefs)
    send_coefs(1)
    for h in range(1, PARTS):
        send_back(h, lambda: None)

    def ready_quads(quads, carry):
        alpha, beta = two(coef_rows[1, :, :NODES]), two(coef_rows[1, :, NODES:])
        for i in quads:
            start = rhs_ref[:, window(i)]
            left = residual_ref[:, window(i)]
            direction = left + beta * start
            step = alpha * direction
            solution_ref[:, window(i)] = coef_rows[0] * start + step
            residual_ref[:, window(i)] = left - two(noise_rows[...]) * step
        return carry

    def final_quads(quads, carry):
        alpha = two(coef_rows[1, :, :NODES])
        for i, back in zip(quads, gather_back(quads)):
            residual_ref[:, window(i)] = residual_ref[:, window(i)] - alpha * back
        return carry

    for h in range(PARTS):
        receive_part(h)
        if h == 0:
            receive_coefs(1)
            for p in range(PARTS):
                over_part(p, ready_quads, 0)
        over_part(h, final_quads, 0)

    for h in range(PARTS):
        done(out_buf.at[h, rest], out_sem.at[h])
        done(ret_buf.at[h, rest], ret_sem.at[h])
    done(stat_out.at[rest], small_sem.at[0])
    for step in range(2):
        done(coef_in.at[step, rest], small_sem.at[1 + step])
    done(places.at[rest], small_sem.at[3])
    done(turn.at[pl.ds(0, (CHIPS - 1) * 4)], small_sem.at[4])
    done(all_b.at[0, pl.ds(1, SIDE - 1)], small_sem.at[5])


def on_device(rhs, tile_weights, tile_owner, tile_row, axis_a, axis_b, coupling, noise):
    tile_count, tile_obs, node_cols = tile_weights.shape
    columns, width = rhs.shape
    a_rows, lvl_here, grid_first = axis_a.shape
    anywhere = pl.BlockSpec(memory_space=pltpu.HBM)
    vmem = pl.BlockSpec(memory_space=pltpu.VMEM)
    smem = pl.BlockSpec(memory_space=pltpu.SMEM)
    dma = pltpu.SemaphoreType.DMA
    whole = pltpu.VMEM((columns, width), F32)
    parts = pltpu.VMEM((PARTS, CHIPS, PART, NODES), BF16)
    field = pltpu.VMEM((LEVELS, GRID_A, NODES), F32)
    return pl.pallas_call(
        kernel,
        out_shape=(whole, whole),
        in_specs=[anywhere, anywhere, vmem, vmem, vmem, vmem, smem, smem],
        out_specs=(vmem, vmem),
        scratch_shapes=[
            whole,
            pltpu.VMEM((tile_count * tile_obs, node_cols), BF16),
            pltpu.VMEM((CHIPS * PITCH, NODES), F32),
            parts,
            parts,
            parts,
            parts,
            pltpu.VMEM((1, TILES), F32),
            pltpu.VMEM((CHIPS, 1, TILES), F32),
            pltpu.VMEM((PARTS, CHIPS // 2, 1, NODES), F32),
            pltpu.VMEM((CHIPS, TILES, NODES), F32),
            pltpu.VMEM((2, SIDE, SIDE * SIDE, a_rows, grid_first), BF16),
            pltpu.VMEM((2, SIDE, NODES, NODES), BF16),
            pltpu.VMEM((LEVELS, GRID_A, GRID_A), BF16),
            field,
            pltpu.VMEM((LEVELS, GRID_A, NODES), BF16),
            field,
            pltpu.VMEM((2, LEVELS, GRID_A, NODES), BF16),
            pltpu.VMEM((LEVELS * GRID_A, NODES), BF16),
            pltpu.VMEM((LEVELS, GRID_A, NODES), BF16),
            pltpu.VMEM((CHIPS, NODES), F32),
            pltpu.VMEM((CHIPS, 1, 2 * NODES), F32),
            pltpu.VMEM((CHIPS, 1, 2 * NODES), F32),
            pltpu.VMEM((2, 1, 2 * NODES), F32),
            pltpu.VMEM((2, 1, 2 * NODES), F32),
            pltpu.VMEM((2, 1, 2 * NODES), F32),
            pltpu.VMEM((2, CHIPS, 1, 2 * NODES), F32),
            pltpu.VMEM((2, CHIPS, 2 * NODES), F32),
            dma((2, PARTS)),
            dma((PARTS,)),
            dma((PARTS, GROUPS)),
            dma((PARTS,)),
            dma((PARTS, GROUPS)),
            dma,
            dma,
            dma,
            dma((2,)),
            dma((8,)),
            dma,
            dma((2,)),
            dma((2, LEVELS)),
            dma((2, LEVELS)),
            dma((2,)),
            dma((2,)),
        ],
        compiler_params=pltpu.CompilerParams(
            collective_id=0, has_side_effects=True, vmem_limit_bytes=59 << 20
        ),
        name="conjugate_gradients",
    )(
        rhs,
        tile_weights.reshape(tile_count * tile_obs, node_cols),
        tile_owner.reshape(1, tile_count),
        tile_row.reshape(1, tile_count),
        axis_a.reshape(a_rows, grid_first),
        axis_b.reshape(node_cols, node_cols),
        coupling,
        noise,
    )


def solution(mesh):
    split = Mesh(mesh.devices.reshape(SIDE, SIDE, SIDE, 2), AXES)
    in_specs = (
        P(None, AXES),
        P(AXES, None, None),
        P(AXES, None),
        P(AXES),
        P(OBS, LVL, None),
        P(LVL, None, None),
        P(),
        P(),
    )
    out_specs = (P(None, AXES), P(None, AXES))
    return jax.shard_map(
        on_device, mesh=split, in_specs=in_specs, out_specs=out_specs, check_vma=False
    )
```
